512 devices in a mesh: region: 32 (over z, core), group: 16 (over x, y).
Axes of the slice: x: 4, y: 4, z: 16, core: 2. Of those that a mesh axis runs over, the one named last changes fastest.
Arguments:
- features: bfloat16 [196608, 2048], P(('region', 'group')), may hold values from -1.5 to 1.5
- memory: bfloat16 [65536, 2048], P(('region', 'group')), may hold values from -1 to 1
- requests: int32 [512, 8], P(('region', 'group')), may hold values from 0 to 15, as said below
- owners: int32 [32, 16], P('region'), may hold values from 0 to 15, as said below
- labels: int32 [512, 384], P(('region', 'group')), may hold values from 0 to 4095, as said below
Outputs:
- feat_grad: bfloat16 [196608, 2048], P(('region', 'group'))
- new_memory: bfloat16 [65536, 2048], P(('region', 'group'))
The draws below stay inside these ranges and needn't reach their ends.
Inputs may be any that keep to these rules, and one draw needn't show every extreme that they name: `owners`: each row of a region is a permutation. `requests`: the 8 numbers of a device are distinct blocks of its region. At most 24 crops of one device carry labels of one region, and every device reaches that bound for some region.
All inputs are finite; a program needn't handle non-finite values.
Results may differ from the reference program's by a relative error of at most 0.006.
Values may be sent and summed in bfloat16 or wider, within the bound.
A program may use at most 64 MiB of HBM per device.

```python
import jax
import jax.numpy as jnp
from jax import lax

D = 2048
BLOCK = 128
BATCH = 384
REGIONS = 32
GROUPW = 16
NB = 8
CAPR = 24
TOTAL = 196608
MEMROWS = 65536
DEVICES = 512


def memory_rows(key, row_list):
    base_key = jax.random.fold_in(key, 101)
    signs = jax.vmap(lambda row: jax.random.rademacher(jax.random.fold_in(base_key, row), (D,), dtype=jnp.float32))(row_list)
    return signs * D ** (-0.5)


def owner_table(key):
    base_key = jax.random.fold_in(key, 202)
    return jax.vmap(lambda region: jax.random.permutation(jax.random.fold_in(base_key, region), GROUPW))(jnp.arange(REGIONS)).astype(jnp.int32)


def request_table(key):
    heat_key = jax.random.fold_in(key, 303)
    pick_key = jax.random.fold_in(key, 304)

    def one_device(device):
        region = device // GROUPW
        heated = (jax.random.randint(jax.random.fold_in(heat_key, region), (GROUPW,), 0, 4) == 0).astype(jnp.int32)
        score = jax.random.randint(jax.random.fold_in(pick_key, device), (GROUPW,), 0, 64) + 64 * heated
        score = score * GROUPW + jnp.arange(GROUPW, dtype=jnp.int32)
        _, chosen = lax.top_k(score, NB)
        return chosen.astype(jnp.int32)
    return jax.vmap(one_device)(jnp.arange(DEVICES))


def draw_memory(key, part):
    return memory_rows(key, jnp.arange(MEMROWS)).astype(jnp.bfloat16)


def draw_owners(key, part):
    return owner_table(key)


def draw_requests(key, part):
    return request_table(key)


def draw_labels(key, part):
    perm_key = jax.random.fold_in(key, 505)
    heat_key = jax.random.fold_in(key, 506)
    shuffle_key = jax.random.fold_in(key, 507)
    row_key = jax.random.fold_in(key, 508)

    def one_device(device):
        order_rank = jax.random.permutation(jax.random.fold_in(perm_key, device), REGIONS * CAPR).astype(jnp.int32)
        heated = jax.random.randint(jax.random.fold_in(heat_key, device), (), 0, REGIONS)
        slot_region = jnp.arange(REGIONS * CAPR, dtype=jnp.int32) // CAPR
        priority = jnp.where(slot_region == heated, -1, order_rank)
        chosen = jnp.argsort(priority, stable=True)[:BATCH].astype(jnp.int32)
        mixing = jax.random.permutation(jax.random.fold_in(shuffle_key, device), BATCH)
        regions_of = chosen[mixing] // CAPR
        rows_of = jax.random.randint(jax.random.fold_in(row_key, device), (BATCH,), 0, BLOCK)
        return (regions_of * BLOCK + rows_of).astype(jnp.int32)
    return jax.vmap(one_device)(jnp.arange(DEVICES))


def draw_features(key, part):
    normal_part = jax.random.normal(jax.random.fold_in(key, 404), (TOTAL, D), jnp.float32)
    normal_part = jnp.clip(normal_part, -6.0, 6.0) * D ** (-0.5)
    return normal_part.astype(jnp.bfloat16)


def setup_inputs(seed: int = 0) -> dict:
    splits = jax.random.split(jax.random.key(seed), 6)
    return {
        "features": draw_features(jax.random.fold_in(splits[5], 71), 0),
        "memory": draw_memory(jax.random.fold_in(splits[5], 71), 0),
        "requests": draw_requests(jax.random.fold_in(splits[5], 71), 0),
        "owners": draw_owners(jax.random.fold_in(splits[5], 71), 0),
        "labels": draw_labels(jax.random.fold_in(splits[5], 71), 0),
    }


exponent_sharpness = 0.05
smoothing = 0.1
momentum_keep = 0.2

def device_grad(index, features, memory, requests, owners):
    region_index = index // GROUPW
    embedding_entries = lax.dynamic_slice_in_dim(features, (index * BATCH).astype(jnp.int32), BATCH, 0)
    wanted_owner = jnp.take(owners[region_index], requests[index], axis=0).astype(jnp.int32)
    row_ids = ((region_index * GROUPW + wanted_owner)[:, None] * BLOCK + jnp.arange(BLOCK, dtype=jnp.int32)[None, :]).reshape(-1)
    reciprocal_memory_slices = jnp.take(memory, row_ids.astype(jnp.int32), axis=0)
    cosine_affinities = jnp.dot(embedding_entries, reciprocal_memory_slices.T, preferred_element_type=jnp.float32) / exponent_sharpness
    shifted = cosine_affinities - lax.optimization_barrier(jnp.max(cosine_affinities, axis=1, keepdims=True))
    expo = jnp.exp(shifted)
    normalized_likelihoods = expo / lax.optimization_barrier(jnp.sum(expo, axis=1, keepdims=True))
    column = jnp.arange(NB * BLOCK, dtype=jnp.int32)
    smoothed_identity_weights = (jnp.where(column < BLOCK, (1.0 - smoothing) / BLOCK, 0.0) + smoothing / (NB * BLOCK)).astype(jnp.float32)
    pre_normalized_derivative = ((normalized_likelihoods - smoothed_identity_weights[None, :]) / exponent_sharpness).astype(jnp.bfloat16)
    return jnp.dot(pre_normalized_derivative, reciprocal_memory_slices, preferred_element_type=jnp.float32).astype(jnp.bfloat16)

def reference(features, memory, requests, owners, labels):
    grads = lax.map(lambda index: device_grad(index, features, memory, requests, owners), jnp.arange(DEVICES, dtype=jnp.int32))
    feat_grad = grads.reshape(TOTAL, D)
    device_of = jnp.arange(TOTAL, dtype=jnp.int32) // BATCH
    group_of = device_of % GROUPW
    flat_labels = labels.reshape(-1).astype(jnp.int32)
    target_row = (flat_labels // BLOCK * GROUPW + group_of) * BLOCK + flat_labels % BLOCK
    sums = jax.ops.segment_sum(features.astype(jnp.float32), target_row, num_segments=MEMROWS)
    counts = jax.ops.segment_sum(jnp.ones((TOTAL,), jnp.float32), target_row, num_segments=MEMROWS)
    old_rows = memory.astype(jnp.float32)
    averaged = sums / jnp.maximum(counts, 1.0)[:, None]
    mixed = jnp.where(counts[:, None] > 0, momentum_keep * old_rows + (1.0 - momentum_keep) * averaged, old_rows)
    scale = lax.rsqrt(lax.optimization_barrier(jnp.mean(mixed * mixed, axis=1, keepdims=True)) + 1e-06) * D ** (-0.5)
    new_memory = (mixed * scale).astype(jnp.bfloat16)
    return (feat_grad, new_memory)
```

```python
import functools

import jax
import jax.numpy as jnp
from jax import lax
from jax.experimental import pallas as pl
from jax.experimental.pallas import tpu as pltpu
from jax.sharding import PartitionSpec as P

MESH = pl.DeviceIdType.MESH
F32 = jnp.float32
BF16 = jnp.bfloat16

SHARPNESS = 0.05
SMOOTHING = 0.1
KEEP = 0.2


def kernel(
    chips, side,
    feat_hbm, mem_hbm, req_ref, own_ref, lab_ref,
    grad_hbm, new_hbm,
    feat, halves, ring, pair, labs, gath, old, part, hits, cand, score, logit, grad, mix, new,
    ring_send, ring_recv, lab_send, lab_recv, sib_send, sib_recv, ag_send, ag_recv, loc,
):
    crops, width = feat.shape
    half = width // 2
    rows = old.shape[1]
    long_arm = chips // 2
    region = lax.axis_index("region")
    group = lax.axis_index("group")
    chip = region // 2
    core = region % 2
    other = 1 - core
    sign = 1 - 2 * core
    gx, gy = group // side, group % side

    def chip_at(offset):
        return (chip + offset + chips) % chips

    def dev(chip_index, core_index, group_index):
        return (chip_index * 2 + core_index, group_index)

    my_cols = pl.ds(pl.multiple_of(core * half, half), half)
    other_cols = pl.ds(pl.multiple_of(other * half, half), half)

    local = [
        pltpu.make_async_copy(feat_hbm.at[:, my_cols], halves.at[0, pl.ds(0, crops)], loc.at[0]),
        pltpu.make_async_copy(feat_hbm.at[:, other_cols], halves.at[1, pl.ds(0, crops)], loc.at[1]),
        pltpu.make_async_copy(feat_hbm, feat, loc.at[2]),
        pltpu.make_async_copy(mem_hbm.at[:, my_cols], old.at[0], loc.at[3]),
        pltpu.make_async_copy(mem_hbm.at[:, other_cols], old.at[1], loc.at[4]),
        pltpu.make_async_copy(mem_hbm, gath.at[group], loc.at[5]),
    ]
    for copy in local:
        copy.start()
    pair[0] = lab_ref[...]

    def at_xy(dx, dy):
        return ((gx + dx + side) % side) * side + (gy + dy + side) % side

    partners = [dev(chip, other, group)]
    for step in (1, -1):
        partners.append(dev(chip_at(step), core, group))
        partners.append(dev(chip_at(step), other, group))
        partners.append((region, at_xy(step, 0)))
        partners.append((region, at_xy(0, step)))
    barrier = pltpu.get_barrier_semaphore()
    for partner in partners:
        pl.semaphore_signal(barrier, inc=1, device_id=partner, device_id_type=MESH)
    pl.semaphore_wait(barrier, len(partners))

    def remote(src, dst, send, recv, device):
        return pltpu.make_async_remote_copy(
            src_ref=src, dst_ref=dst, send_sem=send, recv_sem=recv, device_id=device, device_id_type=MESH
        )

    sibling = dev(chip, other, group)
    swap = [
        remote(pair.at[0], pair.at[1], sib_send.at[0], sib_recv.at[0], sibling),
        remote(feat_hbm.at[:, other_cols], halves.at[0, pl.ds(crops, crops)], sib_send.at[1], sib_recv.at[1], sibling),
        remote(feat_hbm.at[:, my_cols], halves.at[1, pl.ds(crops, crops)], sib_send.at[2], sib_recv.at[2], sibling),
    ]
    for copy in swap:
        copy.start()

    offs = (0, -1, 1, 2)

    def block(h, i, j):
        def off(k):
            return k
        dx, dy = (i, j) if h == 0 else (j, i)
        return at_xy(dx, dy)

    def ag_copy(h, index, src_block, rows_of, device_block, own=False):
        cols = pl.ds(h * half, half)
        dst = gath.at[src_block, rows_of, cols]
        src = mem_hbm.at[rows_of, cols] if own else dst
        return remote(src, dst, ag_send.at[h, index], ag_recv.at[h, index], (region, device_block))

    full = pl.ds(0, rows)
    part_of = {1: pl.ds(0, rows // 2), -1: pl.ds(rows // 2, rows // 2)}
    way = {1: 0, -1: 1}

    def p1(h, u, recv=False):
        return ag_copy(h, way[u], block(h, -u, 0) if recv else block(h, 0, 0), full, block(h, u, 0), own=not recv)

    def p2(h, u, recv=False):
        return ag_copy(h, 2 + way[u], block(h, -2 * u if recv else -u, 0), part_of[u], block(h, u, 0))

    def q1(h, a, u, recv=False):
        return ag_copy(
            h, 4 + 2 * a + way[u], block(h, offs[a], -u if recv else 0), full, block(h, 0, u), own=(a == 0 and not recv)
        )

    def q2(h, a, u, recv=False):
        return ag_copy(
            h, 12 + 2 * a + way[u], block(h, offs[a], -2 * u if recv else -u), part_of[u], block(h, 0, u)
        )

    both = (1, -1)

    def gather_round0():
        for u in both:
            for h in range(2):
                p1(h, u).start()
        for u in both:
            for h in range(2):
                q1(h, 0, u).start()

    def gather_round1():
        for h in range(2):
            for u, a in ((1, 1), (-1, 2)):
                p1(h, u, True).wait_recv()
                p2(h, u).start()
                for v in both:
                    q1(h, a, v).start()
        for h in range(2):
            for u in both:
                q1(h, 0, u, True).wait_recv()
                q2(h, 0, u).start()

    def gather_round2():
        for h in range(2):
            for u in both:
                p2(h, u, True).wait_recv()
            for u in both:
                q1(h, 3, u).start()
        for h in range(2):
            for a in (1, 2):
                for u in both:
                    q1(h, a, u, True).wait_recv()
                    q2(h, a, u).start()

    def gather_round3():
        for h in range(2):
            for u in both:
                q1(h, 3, u, True).wait_recv()
                q2(h, 3, u).start()

    def gather_round4():
        for h in range(2):
            for a in range(4):
                for u in both:
                    q2(h, a, u, True).wait_recv()
        local[5].wait()

    def gather_sent():
        for h in range(2):
            for u in both:
                p1(h, u).wait_send()
                p2(h, u).wait_send()
                for a in range(4):
                    q1(h, a, u).wait_send()
                    q2(h, a, u).wait_send()

    gather_round0()

    places = lax.broadcasted_iota(jnp.int32, (rows, crops), 0)

    def hit(label_row, target):
        return jnp.where(places == label_row - target * rows, 1.0, 0.0)

    def own_sums(target, which):
        pick = jnp.concatenate([hit(pair[0], target), hit(pair[1], target)], axis=1).astype(BF16)
        return jnp.dot(pick, halves[which], preferred_element_type=F32)

    def count(label_pair):
        hits[...] += hit(label_pair[0], region) + hit(label_pair[1], region)

    def ring_copy(t, arm, e, device):
        return remote(
            ring.at[arm, e, t], ring.at[arm, e, t + 1], ring_send.at[arm, e, t], ring_recv.at[arm, e, t + 1], device
        )

    def ring_target(t, arm, e):
        towards = sign * (1 - 2 * arm)
        distance = long_arm - arm - t
        goal = chip_at(towards * distance) * 2 + core + e * sign
        last = (t + arm) // (long_arm - 1)
        nearest = dev(chip_at(towards), core + last * e * sign, group)
        return goal, nearest

    def lab_copy(t, arm):
        towards = sign * (1 - 2 * arm)
        return remote(
            labs.at[arm, t], labs.at[arm, t + 1], lab_send.at[arm, t], lab_recv.at[arm, t + 1],
            dev(chip_at(towards), core, group),
        )

    swap[0].wait_recv()
    for arm in range(2):
        labs[arm, 0] = pair[...]
        lab_copy(0, arm).start()
    local[0].wait()
    swap[1].wait_recv()

    @pl.loop(0, 4)
    def _(q):
        arm, e = q % 2, q // 2
        goal, nearest = ring_target(0, arm, e)
        ring[arm, e, 0] = own_sums(goal, 0).astype(BF16)
        ring_copy(0, arm, e, nearest).start()

    hits[...] = jnp.zeros_like(hits)
    count(pair)

    def take_candidates():
        for k in range(8):
            cand[k * rows:(k + 1) * rows, :] = gath[own_ref[0, req_ref[0, k]]]

    def scores():
        local[2].wait()

        @pl.loop(0, 4)
        def _(n):
            span = pl.ds(pl.multiple_of(n * 256, 256), 256)
            score[:, span] = lax.dot_general(
                feat[...], cand[span, :], (((1,), (1,)), ((), ())), preferred_element_type=F32
            ) * (1.0 / SHARPNESS)

    def softmax():
        total = cand.shape[0]

        @pl.loop(0, crops // 64)
        def _(n):
            span = pl.ds(pl.multiple_of(n * 64, 64), 64)
            s = score[span, :]
            expo = jnp.exp(s - jnp.max(s, axis=1, keepdims=True))
            prob = expo / jnp.sum(expo, axis=1, keepdims=True)
            column = lax.broadcasted_iota(jnp.int32, s.shape, 1)
            target = jnp.where(column < rows, (1.0 - SMOOTHING) / rows, 0.0) + SMOOTHING / total
            logit[span, :] = ((prob - target) * (1.0 / SHARPNESS)).astype(BF16)

    def grads():
        @pl.loop(0, width // 256)
        def _(n):
            span = pl.ds(pl.multiple_of(n * 256, 256), 256)
            grad[:, span] = jnp.dot(logit[...], cand[:, span], preferred_element_type=F32).astype(BF16)

    grad_out = pltpu.make_async_copy(grad, grad_hbm, loc.at[6])

    @pl.loop(1, long_arm)
    def _(t):
        @pl.loop(0, 4)
        def _(q):
            arm, e = q % 2, q // 2

            @pl.when(t + arm < long_arm)
            def _():
                goal, nearest = ring_target(t, arm, e)
                part[...] = own_sums(goal, 0)
                ring_copy(t - 1, arm, e, nearest).wait_recv()
                ring[arm, e, t] = (part[...] + ring[arm, e, t].astype(F32)).astype(BF16)
                ring_copy(t, arm, e, nearest).start()

        for arm in range(2):
            @pl.when(t + arm < long_arm)
            def _():
                lab_copy(t - 1, arm).wait_recv()
                lab_copy(t, arm).start()
                count(labs.at[arm, t])

        @pl.when(t == 1)
        def _():
            gather_round1()

        @pl.when(t == 2)
        def _():
            gather_round2()

        @pl.when(t == 3)
        def _():
            gather_round3()

        @pl.when(t == 4)
        def _():
            gather_round4()
            take_candidates()

        @pl.when(t == 5)
        def _():
            scores()
            softmax()

        @pl.when(t == 6)
        def _():
            grads()
            grad_out.start()

    lab_copy(long_arm - 1, 0).wait_recv()
    count(labs.at[0, long_arm])
    lab_copy(long_arm - 2, 1).wait_recv()
    count(labs.at[1, long_arm - 1])
    counts = jnp.sum(hits[...], axis=1, keepdims=True)
    inverse = 1.0 / jnp.maximum(counts, 1.0)
    local[1].wait()
    swap[2].wait_recv()
    local[3].wait()
    local[4].wait()
    square = jnp.zeros((rows, 1), F32)
    for which in range(2):
        part[...] = own_sums(region, which)
        for arm in range(2):
            ring_copy(long_arm - 1 - arm, arm, which, sibling).wait_recv()
        sums = part[...] + ring[0, which, long_arm].astype(F32) + ring[1, which, long_arm - 1].astype(F32)
        before = old[which].astype(F32)
        mixed = jnp.where(counts > 0, KEEP * before + (1.0 - KEEP) * (sums * inverse), before)
        mix[which] = mixed
        square += jnp.sum(mixed * mixed, axis=1, keepdims=True)
    scale = lax.rsqrt(square * (1.0 / width) + 1e-06) * width ** (-0.5)
    outs = []
    for which, cols in ((0, my_cols), (1, other_cols)):
        new[which] = (mix[which] * scale).astype(BF16)
        copy = pltpu.make_async_copy(new.at[which], new_hbm.at[:, cols], loc.at[7 + which])
        copy.start()
        outs.append(copy)

    for copy in swap:
        copy.wait_send()
    gather_sent()
    for arm in range(2):
        @pl.loop(0, long_arm - arm)
        def _(t):
            lab_copy(t, arm).wait_send()
            for e in range(2):
                ring_copy(t, arm, e, sibling).wait_send()
    grad_out.wait()
    for copy in outs:
        copy.wait()


def solution(mesh):
    regions, groups = mesh.shape["region"], mesh.shape["group"]
    chips = regions // 2
    side = int(round(groups ** 0.5))

    def on_device(features, memory, requests, owners, labels):
        crops, width = features.shape
        rows = memory.shape[0]
        half = width // 2
        arm = chips // 2
        total = requests.shape[1] * rows
        any_spec = pl.BlockSpec(memory_space=pl.ANY)
        smem = pl.BlockSpec(memory_space=pltpu.SMEM)
        vmem = pl.BlockSpec(memory_space=pltpu.VMEM)
        dma = pltpu.SemaphoreType.DMA
        return pl.pallas_call(
            functools.partial(kernel, chips, side),
            out_shape=(
                jax.ShapeDtypeStruct((crops, width), BF16),
                jax.ShapeDtypeStruct((rows, width), BF16),
            ),
            in_specs=[any_spec, any_spec, smem, smem, vmem],
            out_specs=(any_spec, any_spec),
            scratch_shapes=[
                pltpu.VMEM((crops, width), BF16),
                pltpu.VMEM((2, 2 * crops, half), BF16),
                pltpu.VMEM((2, 2, arm + 1, rows, half), BF16),
                pltpu.VMEM((2, 1, crops), jnp.int32),
                pltpu.VMEM((2, arm + 1, 2, 1, crops), jnp.int32),
                pltpu.VMEM((groups, rows, width), BF16),
                pltpu.VMEM((2, rows, half), BF16),
                pltpu.VMEM((rows, half), F32),
                pltpu.VMEM((rows, crops), F32),
                pltpu.VMEM((total, width), BF16),
                pltpu.VMEM((crops, total), F32),
                pltpu.VMEM((crops, total), BF16),
                pltpu.VMEM((crops, width), BF16),
                pltpu.VMEM((2, rows, half), F32),
                pltpu.VMEM((2, rows, half), BF16),
                dma((2, 2, arm + 1)),
                dma((2, 2, arm + 1)),
                dma((2, arm + 1)),
                dma((2, arm + 1)),
                dma((3,)),
                dma((3,)),
                dma((2, 20)),
                dma((2, 20)),
                dma((9,)),
            ],
            compiler_params=pltpu.CompilerParams(
                collective_id=0, has_side_effects=True, vmem_limit_bytes=56 << 20
            ),
        )(features, memory, requests, owners, labels)

    both = P(("region", "group"), None)
    return jax.shard_map(
        on_device,
        mesh=mesh,
        in_specs=(both, both, both, P("region", None), both),
        out_specs=(both, both),
        check_vma=False,
    )
```

```python
import functools

import jax
import jax.numpy as jnp
from jax import lax
from jax.experimental import pallas as pl
from jax.experimental.pallas import tpu as pltpu
from jax.sharding import PartitionSpec as P

MESH = pl.DeviceIdType.MESH
F32 = jnp.float32
BF16 = jnp.bfloat16

SHARPNESS = 0.05
SMOOTHING = 0.1
KEEP = 0.2


def kernel(
    chips, side,
    feat_hbm, mem_hbm, req_ref, own_ref, lab_ref,
    grad_hbm, new_hbm,
    feat, halves, ring, packs, near, far, pair, labs, gath, old, part, hits, cand, score, logit, grad, mix, new,
    ring_send, ring_recv, pack_send, pack_recv, lab_send, lab_recv, sib_send, sib_recv, ag_send, ag_recv, loc,
):
    crops, width = feat.shape
    half = width // 2
    rows = old.shape[1]
    packed = near.shape[1] // 2
    slots = packed // 2
    long_arm = chips // 2
    region = lax.axis_index("region")
    group = lax.axis_index("group")
    chip = region // 2
    core = region % 2
    other = 1 - core
    sign = 1 - 2 * core
    gx, gy = group // side, group % side

    def chip_at(offset):
        return (chip + offset + chips) % chips

    def dev(chip_index, core_index, group_index):
        return (chip_index * 2 + core_index, group_index)

    my_cols = pl.ds(pl.multiple_of(core * half, half), half)
    other_cols = pl.ds(pl.multiple_of(other * half, half), half)

    local = [
        pltpu.make_async_copy(feat_hbm.at[:, my_cols], halves.at[0, pl.ds(0, crops)], loc.at[0]),
        pltpu.make_async_copy(feat_hbm.at[:, other_cols], halves.at[1, pl.ds(0, crops)], loc.at[1]),
        pltpu.make_async_copy(feat_hbm, feat, loc.at[2]),
        pltpu.make_async_copy(mem_hbm.at[:, my_cols], old.at[0], loc.at[3]),
        pltpu.make_async_copy(mem_hbm.at[:, other_cols], old.at[1], loc.at[4]),
        pltpu.make_async_copy(mem_hbm, gath.at[group], loc.at[5]),
    ]
    for copy in local:
        copy.start()

    label = lab_ref[...]
    label_region = lax.shift_right_logical(label, jnp.int32(rows.bit_length() - 1))
    of_region = jnp.where(
        lax.broadcasted_iota(jnp.int32, (2 * chips, crops), 0) == label_region, 1.0, 0.0
    )
    before_crop = jnp.where(
        lax.broadcasted_iota(jnp.int32, (crops, crops), 0) < lax.broadcasted_iota(jnp.int32, (crops, crops), 1),
        1.0, 0.0,
    ).astype(BF16)
    earlier = jnp.dot(of_region.astype(BF16), before_crop, preferred_element_type=F32)
    rank = jnp.sum(earlier * of_region, axis=0, keepdims=True).astype(jnp.int32)
    pair[0, :, 0:crops] = label
    pair[0, :, crops:2 * crops] = label_region * slots + rank

    def at_xy(dx, dy):
        return ((gx + dx + side) % side) * side + (gy + dy + side) % side

    partners = [dev(chip, other, group)]
    for step in (1, -1):
        partners.append(dev(chip_at(step), core, group))
        partners.append(dev(chip_at(step), other, group))
        partners.append((region, at_xy(step, 0)))
        partners.append((region, at_xy(0, step)))
    barrier = pltpu.get_barrier_semaphore()
    for partner in partners:
        pl.semaphore_signal(barrier, inc=1, device_id=partner, device_id_type=MESH)
    pl.semaphore_wait(barrier, len(partners))

    def remote(src, dst, send, recv, device):
        return pltpu.make_async_remote_copy(
            src_ref=src, dst_ref=dst, send_sem=send, recv_sem=recv, device_id=device, device_id_type=MESH
        )

    sibling = dev(chip, other, group)
    swap = [
        remote(pair.at[0], pair.at[1], sib_send.at[0], sib_recv.at[0], sibling),
        remote(feat_hbm.at[:, other_cols], halves.at[0, pl.ds(crops, crops)], sib_send.at[1], sib_recv.at[1], sibling),
        remote(feat_hbm.at[:, my_cols], halves.at[1, pl.ds(crops, crops)], sib_send.at[2], sib_recv.at[2], sibling),
    ]
    swap[0].start()

    def pack_copy(stage, arm, e):
        towards = sign * (1 - 2 * arm) * (1 - 2 * e)
        place = pl.ds(pl.multiple_of(e * packed, packed), packed)
        landing = near if stage == 0 else far
        return remote(
            packs.at[stage, arm, e], landing.at[arm, place],
            pack_send.at[arm, 2 * stage + e], pack_recv.at[arm, 2 * stage + e],
            dev(chip_at(towards), core + e * sign, group),
        )

    def forward_copy(arm):
        towards = sign * (1 - 2 * arm)
        return remote(
            near.at[arm], far.at[arm, pl.ds(2 * packed, 2 * packed)], pack_send.at[arm, 4], pack_recv.at[arm, 4],
            dev(chip_at(towards), core, group),
        )

    def send_packed(stage):
        @pl.loop(0, 4)
        def _(q):
            arm, e = q % 2, q // 2
            towards = sign * (1 - 2 * arm) * (1 - 2 * e)
            goal = chip_at(towards * (long_arm - arm - stage))
            take = jnp.where(
                lax.broadcasted_iota(jnp.int32, (packed, crops), 0) + goal * packed == pair[0, :, crops:2 * crops],
                1.0, 0.0,
            ).astype(BF16)
            packs[stage, arm, e] = jnp.dot(
                take, halves[e, 0:crops, :], preferred_element_type=F32
            ).astype(BF16)
            pack_copy(stage, arm, e).start()

    local[0].wait()
    local[1].wait()
    send_packed(0)
    swap[1].start()

    offs = (0, -1, 1, 2)

    def block(h, i, j):
        def off(k):
            return k
        dx, dy = (i, j) if h == 0 else (j, i)
        return at_xy(dx, dy)

    def ag_copy(h, index, src_block, rows_of, device_block, own=False):
        cols = pl.ds(h * half, half)
        dst = gath.at[src_block, rows_of, cols]
        src = mem_hbm.at[rows_of, cols] if own else dst
        return remote(src, dst, ag_send.at[h, index], ag_recv.at[h, index], (region, device_block))

    full = pl.ds(0, rows)
    part_of = {1: pl.ds(0, rows // 2), -1: pl.ds(rows // 2, rows // 2)}
    way = {1: 0, -1: 1}

    def p1(h, u, recv=False):
        return ag_copy(h, way[u], block(h, -u, 0) if recv else block(h, 0, 0), full, block(h, u, 0), own=not recv)

    def p2(h, u, recv=False):
        return ag_copy(h, 2 + way[u], block(h, -2 * u if recv else -u, 0), part_of[u], block(h, u, 0))

    def q1(h, a, u, recv=False):
        return ag_copy(
            h, 4 + 2 * a + way[u], block(h, offs[a], -u if recv else 0), full, block(h, 0, u), own=(a == 0 and not recv)
        )

    def q2(h, a, u, recv=False):
        return ag_copy(
            h, 12 + 2 * a + way[u], block(h, offs[a], -2 * u if recv else -u), part_of[u], block(h, 0, u)
        )

    both = (1, -1)

    def gather_round0():
        for u in both:
            for h in range(2):
                p1(h, u).start()
        for u in both:
            for h in range(2):
                q1(h, 0, u).start()

    def gather_round1():
        for h in range(2):
            for u, a in ((1, 1), (-1, 2)):
                p1(h, u, True).wait_recv()
                p2(h, u).start()
                for v in both:
                    q1(h, a, v).start()
        for h in range(2):
            for u in both:
                q1(h, 0, u, True).wait_recv()
                q2(h, 0, u).start()

    def gather_round2():
        for h in range(2):
            for u in both:
                p2(h, u, True).wait_recv()
            for u in both:
                q1(h, 3, u).start()
        for h in range(2):
            for a in (1, 2):
                for u in both:
                    q1(h, a, u, True).wait_recv()
                    q2(h, a, u).start()

    def gather_round3():
        for h in range(2):
            for u in both:
                q1(h, 3, u, True).wait_recv()
                q2(h, 3, u).start()

    def gather_round4():
        for h in range(2):
            for a in range(4):
                for u in both:
                    q2(h, a, u, True).wait_recv()
        local[5].wait()

    def gather_sent():
        for h in range(2):
            for u in both:
                p1(h, u).wait_send()
                p2(h, u).wait_send()
                for a in range(4):
                    q1(h, a, u).wait_send()
                    q2(h, a, u).wait_send()

    gather_round0()
    send_packed(1)
    swap[2].start()

    places = lax.broadcasted_iota(jnp.int32, (rows, crops), 0)

    def hit(label_row, target):
        return jnp.where(places == label_row - target * rows, 1.0, 0.0)

    def own_sums(target, which):
        pick = jnp.concatenate([hit(pair[k, :, 0:crops], target) for k in range(2)], axis=1).astype(BF16)
        return jnp.dot(pick, halves[which], preferred_element_type=F32)

    def count(label_pair):
        hits[...] += hit(label_pair[0, :, 0:crops], region) + hit(label_pair[1, :, 0:crops], region)

    def spread(arm, target):
        sources = [(labs.at[arm, hop], k) for hop in (1, 2) for k in range(2)]
        first = target // 2 * packed
        put, take = [], []
        for n, (source, k) in enumerate(sources):
            slot = source[k, :, crops:2 * crops] - first
            slot = jnp.where((slot >= 0) & (slot < packed), slot + n * packed, -1)
            place = lax.broadcasted_iota(jnp.int32, (4 * packed, crops), 0)
            take.append(jnp.where(place == slot, 1.0, 0.0).astype(BF16))
            put.append(hit(source[k, :, 0:crops], target).astype(BF16))
        move = lax.dot_general(
            jnp.concatenate(put, axis=1), jnp.concatenate(take, axis=1), (((1,), (1,)), ((), ())),
            preferred_element_type=F32,
        ).astype(BF16)
        return jnp.dot(move, far[arm], preferred_element_type=F32)

    def ring_copy(t, arm, e, device):
        return remote(
            ring.at[arm, e, t - 2], ring.at[arm, e, t - 1], ring_send.at[arm, e, t - 2], ring_recv.at[arm, e, t - 1],
            device,
        )

    def ring_target(t, arm, e):
        towards = sign * (1 - 2 * arm)
        distance = long_arm - arm - t
        goal = chip_at(towards * distance) * 2 + core + e * sign
        last = (t + arm) // (long_arm - 1)
        nearest = dev(chip_at(towards), core + last * e * sign, group)
        return goal, nearest

    def lab_copy(t, arm):
        towards = sign * (1 - 2 * arm)
        return remote(
            labs.at[arm, t], labs.at[arm, t + 1], lab_send.at[arm, t], lab_recv.at[arm, t + 1],
            dev(chip_at(towards), core, group),
        )

    swap[0].wait_recv()
    for arm in range(2):
        labs[arm, 0] = pair[...]
        lab_copy(0, arm).start()
    hits[...] = jnp.zeros_like(hits)
    count(pair)

    def take_candidates():
        for k in range(8):
            cand[k * rows:(k + 1) * rows, :] = gath[own_ref[0, req_ref[0, k]]]

    def scores():
        local[2].wait()

        @pl.loop(0, 4)
        def _(n):
            span = pl.ds(pl.multiple_of(n * 256, 256), 256)
            score[:, span] = lax.dot_general(
                feat[...], cand[span, :], (((1,), (1,)), ((), ())), preferred_element_type=F32
            ) * (1.0 / SHARPNESS)

    def softmax():
        total = cand.shape[0]

        @pl.loop(0, crops // 64)
        def _(n):
            span = pl.ds(pl.multiple_of(n * 64, 64), 64)
            s = score[span, :]
            expo = jnp.exp(s - jnp.max(s, axis=1, keepdims=True))
            prob = expo / jnp.sum(expo, axis=1, keepdims=True)
            column = lax.broadcasted_iota(jnp.int32, s.shape, 1)
            target = jnp.where(column < rows, (1.0 - SMOOTHING) / rows, 0.0) + SMOOTHING / total
            logit[span, :] = ((prob - target) * (1.0 / SHARPNESS)).astype(BF16)

    def grads():
        @pl.loop(0, width // 256)
        def _(n):
            span = pl.ds(pl.multiple_of(n * 256, 256), 256)
            grad[:, span] = jnp.dot(logit[...], cand[:, span], preferred_element_type=F32).astype(BF16)

    grad_out = pltpu.make_async_copy(grad, grad_hbm, loc.at[6])

    def pass_labels(t, arm):
        lab_copy(t - 1, arm).wait_recv()
        lab_copy(t, arm).start()
        count(labs.at[arm, t])

    for arm in range(2):
        for e in range(2):
            pack_copy(0, arm, e).wait_recv()
        forward_copy(arm).start()
        pass_labels(1, arm)
    gather_round1()
    swap[1].wait_recv()

    for arm in range(2):
        for e in range(2):
            pack_copy(1, arm, e).wait_recv()
        forward_copy(arm).wait_recv()
        pass_labels(2, arm)

    @pl.loop(0, 4)
    def _(q):
        arm, e = q % 2, q // 2
        goal, nearest = ring_target(2, arm, e)
        part[...] = own_sums(goal, 0)
        ring[arm, e, 0] = (part[...] + spread(arm, goal)).astype(BF16)
        ring_copy(2, arm, e, nearest).start()

    gather_round2()

    @pl.loop(3, long_arm)
    def _(t):
        @pl.loop(0, 4)
        def _(q):
            arm, e = q % 2, q // 2

            @pl.when(t + arm < long_arm)
            def _():
                goal, nearest = ring_target(t, arm, e)
                part[...] = own_sums(goal, 0)
                ring_copy(t - 1, arm, e, nearest).wait_recv()
                ring[arm, e, t - 2] = (part[...] + ring[arm, e, t - 2].astype(F32)).astype(BF16)
                ring_copy(t, arm, e, nearest).start()

        for arm in range(2):
            @pl.when(t + arm < long_arm)
            def _():
                pass_labels(t, arm)

        @pl.when(t == 3)
        def _():
            gather_round3()

        @pl.when(t == 4)
        def _():
            gather_round4()
            take_candidates()

        @pl.when(t == 5)
        def _():
            scores()
            softmax()

        @pl.when(t == 6)
        def _():
            grads()
            grad_out.start()

    lab_copy(long_arm - 1, 0).wait_recv()
    count(labs.at[0, long_arm])
    lab_copy(long_arm - 2, 1).wait_recv()
    count(labs.at[1, long_arm - 1])
    counts = jnp.sum(hits[...], axis=1, keepdims=True)
    inverse = 1.0 / jnp.maximum(counts, 1.0)
    swap[2].wait_recv()
    local[3].wait()
    local[4].wait()
    square = jnp.zeros((rows, 1), F32)
    for which in range(2):
        part[...] = own_sums(region, which)
        for arm in range(2):
            ring_copy(long_arm - 1 - arm, arm, which, sibling).wait_recv()
        sums = part[...] + ring[0, which, long_arm - 2].astype(F32) + ring[1, which, long_arm - 3].astype(F32)
        before = old[which].astype(F32)
        mixed = jnp.where(counts > 0, KEEP * before + (1.0 - KEEP) * (sums * inverse), before)
        mix[which] = mixed
        square += jnp.sum(mixed * mixed, axis=1, keepdims=True)
    scale = lax.rsqrt(square * (1.0 / width) + 1e-06) * width ** (-0.5)
    outs = []
    for which, cols in ((0, my_cols), (1, other_cols)):
        new[which] = (mix[which] * scale).astype(BF16)
        copy = pltpu.make_async_copy(new.at[which], new_hbm.at[:, cols], loc.at[7 + which])
        copy.start()
        outs.append(copy)

    for copy in swap:
        copy.wait_send()
    gather_sent()
    for arm in range(2):
        forward_copy(arm).wait_send()
        for e in range(2):
            for stage in range(2):
                pack_copy(stage, arm, e).wait_send()

        @pl.loop(0, long_arm - arm)
        def _(t):
            lab_copy(t, arm).wait_send()

        @pl.loop(2, long_arm - arm)
        def _(t):
            for e in range(2):
                ring_copy(t, arm, e, sibling).wait_send()
    grad_out.wait()
    for copy in outs:
        copy.wait()


def hand_over(grad_in, new_in, grad_out, new_out, sem):
    crops, rows = grad_in.shape[0], new_in.shape[0]
    piece = rows // 2
    copies = []
    for source, target, count in ((grad_in, grad_out, crops), (new_in, new_out, rows)):
        for first in range(0, count, piece):
            span = pl.ds(first, piece)
            copies.append(pltpu.make_async_copy(source.at[span], target.at[span], sem.at[len(copies)]))
    for copy in copies:
        copy.start()
    for copy in copies:
        copy.wait()


def solution(mesh):
    regions, groups = mesh.shape["region"], mesh.shape["group"]
    chips = regions // 2
    side = int(round(groups ** 0.5))

    def on_device(features, memory, requests, owners, labels):
        crops, width = features.shape
        rows = memory.shape[0]
        half = width // 2
        arm = chips // 2
        total = requests.shape[1] * rows
        any_spec = pl.BlockSpec(memory_space=pl.ANY)
        smem = pl.BlockSpec(memory_space=pltpu.SMEM)
        vmem = pl.BlockSpec(memory_space=pltpu.VMEM)
        dma = pltpu.SemaphoreType.DMA
        shapes = (
            jax.ShapeDtypeStruct((crops, width), BF16),
            jax.ShapeDtypeStruct((rows, width), BF16),
        )
        packed = 2 * max(2, 2 * crops // regions)
        results = pl.pallas_call(
            functools.partial(kernel, chips, side),
            out_shape=shapes,
            in_specs=[any_spec, any_spec, smem, smem, vmem],
            out_specs=(any_spec, any_spec),
            scratch_shapes=[
                pltpu.VMEM((crops, width), BF16),
                pltpu.VMEM((2, 2 * crops, half), BF16),
                pltpu.VMEM((2, 2, arm - 1, rows, half), BF16),
                pltpu.VMEM((2, 2, 2, packed, half), BF16),
                pltpu.VMEM((2, 2 * packed, half), BF16),
                pltpu.VMEM((2, 4 * packed, half), BF16),
                pltpu.VMEM((2, 1, 2 * crops), jnp.int32),
                pltpu.VMEM((2, arm + 1, 2, 1, 2 * crops), jnp.int32),
                pltpu.VMEM((groups, rows, width), BF16),
                pltpu.VMEM((2, rows, half), BF16),
                pltpu.VMEM((rows, half), F32),
                pltpu.VMEM((rows, crops), F32),
                pltpu.VMEM((total, width), BF16),
                pltpu.VMEM((crops, total), F32),
                pltpu.VMEM((crops, total), BF16),
                pltpu.VMEM((crops, width), BF16),
                pltpu.VMEM((2, rows, half), F32),
                pltpu.VMEM((2, rows, half), BF16),
                dma((2, 2, arm - 1)),
                dma((2, 2, arm - 1)),
                dma((2, 5)),
                dma((2, 5)),
                dma((2, arm + 1)),
                dma((2, arm + 1)),
                dma((3,)),
                dma((3,)),
                dma((2, 20)),
                dma((2, 20)),
                dma((9,)),
            ],
            compiler_params=pltpu.CompilerParams(
                collective_id=0, has_side_effects=True, vmem_limit_bytes=56 << 20
            ),
        )(features, memory, requests, owners, labels)
        pieces = 2 * (crops + rows) // rows
        return pl.pallas_call(
            hand_over,
            out_shape=shapes,
            in_specs=[any_spec, any_spec],
            out_specs=(any_spec, any_spec),
            scratch_shapes=[dma((pieces,))],
        )(*results)

    both = P(("region", "group"), None)
    return jax.shard_map(
        on_device,
        mesh=mesh,
        in_specs=(both, both, both, P("region", None), both),
        out_specs=(both, both),
        check_vma=False,
    )
```

```python
import functools

import jax
import jax.numpy as jnp
from jax import lax
from jax.experimental import pallas as pl
from jax.experimental.pallas import tpu as pltpu
from jax.sharding import PartitionSpec as P

MESH = pl.DeviceIdType.MESH
F32 = jnp.float32
BF16 = jnp.bfloat16

SHARPNESS = 0.05
SMOOTHING = 0.1
KEEP = 0.2


def kernel(
    chips, side,
    feat_hbm, mem_hbm, req_ref, own_ref, lab_ref,
    grad, new,
    feat, halves, ring, packs, near, far, pair, labs, gath, old, part, move, hits, cand, score, logit, mix,
    ring_send, ring_recv, pack_send, pack_recv, lab_send, lab_recv, sib_send, sib_recv, ag_send, ag_recv, loc,
):
    crops, width = feat.shape
    half = width // 2
    rows = old.shape[1]
    packed = near.shape[1] // 2
    slots = packed // 2
    long_arm = chips // 2
    region = lax.axis_index("region")
    group = lax.axis_index("group")
    chip = region // 2
    core = region % 2
    other = 1 - core
    sign = 1 - 2 * core
    gx, gy = group // side, group % side

    def chip_at(offset):
        return (chip + offset + chips) % chips

    def dev(chip_index, core_index, group_index):
        return (chip_index * 2 + core_index, group_index)

    my_cols = pl.ds(pl.multiple_of(core * half, half), half)
    other_cols = pl.ds(pl.multiple_of(other * half, half), half)

    def at_xy(dx, dy):
        return ((gx + dx + side) % side) * side + (gy + dy + side) % side

    partners = [dev(chip, other, group)]
    for step in (1, -1):
        partners.append(dev(chip_at(step), core, group))
        partners.append(dev(chip_at(step), other, group))
        partners.append((region, at_xy(step, 0)))
        partners.append((region, at_xy(0, step)))
    barrier = pltpu.get_barrier_semaphore()
    for partner in partners:
        pl.semaphore_signal(barrier, inc=1, device_id=partner, device_id_type=MESH)

    local = [
        pltpu.make_async_copy(feat_hbm.at[:, my_cols], halves.at[0, pl.ds(0, crops)], loc.at[0]),
        pltpu.make_async_copy(feat_hbm.at[:, other_cols], halves.at[1, pl.ds(0, crops)], loc.at[1]),
        pltpu.make_async_copy(feat_hbm, feat, loc.at[2]),
        pltpu.make_async_copy(mem_hbm.at[:, my_cols], old.at[0], loc.at[3]),
        pltpu.make_async_copy(mem_hbm.at[:, other_cols], old.at[1], loc.at[4]),
        pltpu.make_async_copy(mem_hbm, gath.at[group], loc.at[5]),
    ]
    for copy in local:
        copy.start()

    label = lab_ref[...]
    label_region = lax.shift_right_logical(label, jnp.int32(rows.bit_length() - 1))
    of_region = jnp.where(
        lax.broadcasted_iota(jnp.int32, (2 * chips, crops), 0) == label_region, 1.0, 0.0
    )
    before_crop = jnp.where(
        lax.broadcasted_iota(jnp.int32, (crops, crops), 0) < lax.broadcasted_iota(jnp.int32, (crops, crops), 1),
        1.0, 0.0,
    ).astype(BF16)
    earlier = jnp.dot(of_region.astype(BF16), before_crop, preferred_element_type=F32)
    rank = jnp.sum(earlier * of_region, axis=0, keepdims=True).astype(jnp.int32)
    pair[0, :, 0:crops] = label
    pair[0, :, crops:2 * crops] = label_region * slots + rank

    pl.semaphore_wait(barrier, len(partners))

    def remote(src, dst, send, recv, device):
        return pltpu.make_async_remote_copy(
            src_ref=src, dst_ref=dst, send_sem=send, recv_sem=recv, device_id=device, device_id_type=MESH
        )

    sibling = dev(chip, other, group)
    swap = [
        remote(pair.at[0], pair.at[1], sib_send.at[0], sib_recv.at[0], sibling),
        remote(feat_hbm.at[:, other_cols], halves.at[0, pl.ds(crops, crops)], sib_send.at[1], sib_recv.at[1], sibling),
        remote(feat_hbm.at[:, my_cols], halves.at[1, pl.ds(crops, crops)], sib_send.at[2], sib_recv.at[2], sibling),
    ]
    swap[0].start()

    def pack_copy(stage, arm, e):
        towards = sign * (1 - 2 * arm) * (1 - 2 * e)
        place = pl.ds(pl.multiple_of(e * packed, packed), packed)
        landing = near if stage == 0 else far
        return remote(
            packs.at[stage, arm, e], landing.at[arm, place],
            pack_send.at[arm, 2 * stage + e], pack_recv.at[arm, 2 * stage + e],
            dev(chip_at(towards), core + e * sign, group),
        )

    def forward_copy(arm):
        towards = sign * (1 - 2 * arm)
        return remote(
            near.at[arm], far.at[arm, pl.ds(2 * packed, 2 * packed)], pack_send.at[arm, 4], pack_recv.at[arm, 4],
            dev(chip_at(towards), core, group),
        )

    def send_packed(stage, arm):
        @pl.loop(0, 2)
        def _(e):
            towards = sign * (1 - 2 * arm) * (1 - 2 * e)
            goal = chip_at(towards * (long_arm - arm - stage))
            take = jnp.where(
                lax.broadcasted_iota(jnp.int32, (packed, crops), 0) + goal * packed == pair[0, :, crops:2 * crops],
                1.0, 0.0,
            ).astype(BF16)
            packs[stage, arm, e] = jnp.dot(
                take, halves[e, 0:crops, :], preferred_element_type=F32
            ).astype(BF16)
            pack_copy(stage, arm, e).start()

    local[0].wait()
    local[1].wait()
    send_packed(0, 0)

    offs = (0, -1, 1, 2)

    def block(h, i, j):
        def off(k):
            return k
        dx, dy = (i, j) if h == 0 else (j, i)
        return at_xy(dx, dy)

    def ag_copy(h, index, src_block, rows_of, device_block, own=False):
        cols = pl.ds(h * half, half)
        dst = gath.at[src_block, rows_of, cols]
        src = mem_hbm.at[rows_of, cols] if own else dst
        return remote(src, dst, ag_send.at[h, index], ag_recv.at[h, index], (region, device_block))

    full = pl.ds(0, rows)
    part_of = {1: pl.ds(0, rows // 2), -1: pl.ds(rows // 2, rows // 2)}
    way = {1: 0, -1: 1}

    def p1(h, u, recv=False):
        return ag_copy(h, way[u], block(h, -u, 0) if recv else block(h, 0, 0), full, block(h, u, 0), own=not recv)

    def p2(h, u, recv=False):
        return ag_copy(h, 2 + way[u], block(h, -2 * u if recv else -u, 0), part_of[u], block(h, u, 0))

    def q1(h, a, u, recv=False):
        return ag_copy(
            h, 4 + 2 * a + way[u], block(h, offs[a], -u if recv else 0), full, block(h, 0, u), own=(a == 0 and not recv)
        )

    def q2(h, a, u, recv=False):
        return ag_copy(
            h, 12 + 2 * a + way[u], block(h, offs[a], -2 * u if recv else -u), part_of[u], block(h, 0, u)
        )

    both = (1, -1)

    def gather_round0():
        for u in both:
            for h in range(2):
                p1(h, u).start()
        for u in both:
            for h in range(2):
                q1(h, 0, u).start()

    def gather_round1():
        for h in range(2):
            for u, a in ((1, 1), (-1, 2)):
                p1(h, u, True).wait_recv()
                p2(h, u).start()
                for v in both:
                    q1(h, a, v).start()

    def gather_round1b():
        for h in range(2):
            for u in both:
                q1(h, 0, u, True).wait_recv()
                q2(h, 0, u).start()

    def gather_round2():
        for h in range(2):
            for u in both:
                p2(h, u, True).wait_recv()
            for u in both:
                q1(h, 3, u).start()
        for h in range(2):
            for a in (1, 2):
                for u in both:
                    q1(h, a, u, True).wait_recv()
                    q2(h, a, u).start()

    def gather_round3():
        for h in range(2):
            for u in both:
                q1(h, 3, u, True).wait_recv()
                q2(h, 3, u).start()

    def gather_round4():
        for h in range(2):
            for a in range(4):
                for u in both:
                    q2(h, a, u, True).wait_recv()
        local[5].wait()

    def gather_sent():
        for h in range(2):
            for u in both:
                p1(h, u).wait_send()
                p2(h, u).wait_send()
                for a in range(4):
                    q1(h, a, u).wait_send()
                    q2(h, a, u).wait_send()

    gather_round0()
    send_packed(1, 0)
    swap[1].start()
    swap[2].start()
    send_packed(0, 1)

    places = lax.broadcasted_iota(jnp.int32, (rows, crops), 0)

    def hit(label_row, target):
        return jnp.where(places == label_row - target * rows, 1.0, 0.0)

    def own_sums(target, which):
        pick = jnp.concatenate([hit(pair[k, :, 0:crops], target) for k in range(2)], axis=1).astype(BF16)
        return jnp.dot(pick, halves[which], preferred_element_type=F32)

    def count(label_pair):
        hits[...] += hit(label_pair[0, :, 0:crops], region) + hit(label_pair[1, :, 0:crops], region)

    def moves(arm, target):
        sources = [(labs.at[arm, hop], k) for hop in (1, 2) for k in range(2)]
        first = target // 2 * packed
        put, take = [], []
        for n, (source, k) in enumerate(sources):
            slot = source[k, :, crops:2 * crops] - first
            slot = jnp.where((slot >= 0) & (slot < packed), slot + n * packed, -1)
            place = lax.broadcasted_iota(jnp.int32, (4 * packed, crops), 0)
            take.append(jnp.where(place == slot, 1.0, 0.0).astype(BF16))
            put.append(hit(source[k, :, 0:crops], target).astype(BF16))
        return lax.dot_general(
            jnp.concatenate(put, axis=1), jnp.concatenate(take, axis=1), (((1,), (1,)), ((), ())),
            preferred_element_type=F32,
        ).astype(BF16)

    def ring_copy(t, arm, e, device):
        return remote(
            ring.at[arm, e, t - 2], ring.at[arm, e, t - 1], ring_send.at[arm, e, t - 2], ring_recv.at[arm, e, t - 1],
            device,
        )

    def ring_target(t, arm, e):
        towards = sign * (1 - 2 * arm)
        distance = long_arm - arm - t
        goal = chip_at(towards * distance) * 2 + core + e * sign
        last = (t + arm) // (long_arm - 1)
        nearest = dev(chip_at(towards), core + last * e * sign, group)
        return goal, nearest

    def lab_copy(t, arm):
        towards = sign * (1 - 2 * arm)
        return remote(
            labs.at[arm, t], labs.at[arm, t + 1], lab_send.at[arm, t], lab_recv.at[arm, t + 1],
            dev(chip_at(towards), core, group),
        )

    swap[0].wait_recv()
    for arm in range(2):
        labs[arm, 0] = pair[...]
        lab_copy(0, arm).start()
    hits[...] = jnp.zeros_like(hits)
    count(pair)

    def take_candidates():
        for k in range(8):
            cand[k * rows:(k + 1) * rows, :] = gath[own_ref[0, req_ref[0, k]]]

    def scores():
        local[2].wait()

        @pl.loop(0, 4)
        def _(n):
            span = pl.ds(pl.multiple_of(n * 256, 256), 256)
            score[:, span] = lax.dot_general(
                feat[...], cand[span, :], (((1,), (1,)), ((), ())), preferred_element_type=F32
            ) * (1.0 / SHARPNESS)

    def softmax():
        total = cand.shape[0]

        @pl.loop(0, crops // 64)
        def _(n):
            span = pl.ds(pl.multiple_of(n * 64, 64), 64)
            s = score[span, :]
            expo = jnp.exp(s - jnp.max(s, axis=1, keepdims=True))
            prob = expo / jnp.sum(expo, axis=1, keepdims=True)
            column = lax.broadcasted_iota(jnp.int32, s.shape, 1)
            target = jnp.where(column < rows, (1.0 - SMOOTHING) / rows, 0.0) + SMOOTHING / total
            logit[span, :] = ((prob - target) * (1.0 / SHARPNESS)).astype(BF16)

    def grads():
        @pl.loop(0, width // 256)
        def _(n):
            span = pl.ds(pl.multiple_of(n * 256, 256), 256)
            grad[:, span] = jnp.dot(logit[...], cand[:, span], preferred_element_type=F32).astype(BF16)

    def pass_labels(t, arm):
        lab_copy(t - 1, arm).wait_recv()
        lab_copy(t, arm).start()
        count(labs.at[arm, t])

    for arm in range(2):
        for e in range(2):
            pack_copy(0, arm, e).wait_recv()
        forward_copy(arm).start()
        if arm == 0:
            send_packed(1, 1)
    for arm in range(2):
        pass_labels(1, arm)
    swap[1].wait_recv()

    for arm in range(2):
        @pl.loop(0, 2)
        def _(e):
            goal, _ = ring_target(2, arm, e)
            part[2 * arm + e] = own_sums(goal, 0)

        if arm == 0:
            gather_round1()
            for k in range(2):
                pass_labels(2, k)

        @pl.loop(0, 2)
        def _(e):
            goal, _ = ring_target(2, arm, e)
            move[2 * arm + e] = moves(arm, goal)

        for e in range(2):
            pack_copy(1, arm, e).wait_recv()
        forward_copy(arm).wait_recv()

        @pl.loop(0, 2)
        def _(e):
            _, nearest = ring_target(2, arm, e)
            come = jnp.dot(move[2 * arm + e], far[arm], preferred_element_type=F32)
            ring[arm, e, 0] = (part[2 * arm + e] + come).astype(BF16)
            ring_copy(2, arm, e, nearest).start()

    gather_round1b()
    for arm in range(2):
        pass_labels(3, arm)

    @pl.loop(3, long_arm)
    def _(t):
        @pl.loop(0, 4)
        def _(q):
            arm, e = q // 2, q % 2

            @pl.when(t + arm < long_arm)
            def _():
                goal, nearest = ring_target(t, arm, e)
                part[0] = own_sums(goal, 0)
                ring_copy(t - 1, arm, e, nearest).wait_recv()
                ring[arm, e, t - 2] = (part[0] + ring[arm, e, t - 2].astype(F32)).astype(BF16)
                ring_copy(t, arm, e, nearest).start()

        for arm in range(2):
            @pl.when(t + arm + 1 < long_arm)
            def _():
                pass_labels(t + 1, arm)

        @pl.when(t == 3)
        def _():
            gather_round2()

        @pl.when(t == 4)
        def _():
            gather_round3()

        @pl.when(t == 5)
        def _():
            gather_round4()
            take_candidates()
            scores()

        @pl.when(t == 6)
        def _():
            softmax()
            grads()

    lab_copy(long_arm - 1, 0).wait_recv()
    count(labs.at[0, long_arm])
    lab_copy(long_arm - 2, 1).wait_recv()
    count(labs.at[1, long_arm - 1])
    counts = jnp.sum(hits[...], axis=1, keepdims=True)
    keep = jnp.where(counts > 0, KEEP, 1.0)
    take = jnp.where(counts > 0, (1.0 - KEEP) / jnp.maximum(counts, 1.0), 0.0)
    swap[2].wait_recv()
    local[3].wait()
    local[4].wait()
    for which in range(2):
        part[0] = own_sums(region, which)
        ring_copy(long_arm - 2, 1, which, sibling).wait_recv()
        mix[which] = keep * old[which].astype(F32) + take * (part[0] + ring[1, which, long_arm - 3].astype(F32))
    square = jnp.zeros((rows, 1), F32)
    for which in range(2):
        ring_copy(long_arm - 1, 0, which, sibling).wait_recv()
        mixed = mix[which] + take * ring[0, which, long_arm - 2].astype(F32)
        mix[which] = mixed
        square += jnp.sum(mixed * mixed, axis=1, keepdims=True)
    scale = lax.rsqrt(square * (1.0 / width) + 1e-06) * width ** (-0.5)
    for which, cols in ((0, my_cols), (1, other_cols)):
        new[:, cols] = (mix[which] * scale).astype(BF16)

    for copy in swap:
        copy.wait_send()
    gather_sent()
    for arm in range(2):
        forward_copy(arm).wait_send()
        for e in range(2):
            for stage in range(2):
                pack_copy(stage, arm, e).wait_send()

        @pl.loop(0, long_arm - arm)
        def _(t):
            lab_copy(t, arm).wait_send()

        @pl.loop(2, long_arm - arm)
        def _(t):
            for e in range(2):
                ring_copy(t, arm, e, sibling).wait_send()


def hand_over(grad, new, grad_out, new_out, sem):
    copies = [
        pltpu.make_async_copy(grad, grad_out, sem.at[0]),
        pltpu.make_async_copy(new, new_out, sem.at[1]),
    ]
    for copy in copies:
        copy.start()
    for copy in copies:
        copy.wait()


def solution(mesh):
    regions, groups = mesh.shape["region"], mesh.shape["group"]
    chips = regions // 2
    side = int(round(groups ** 0.5))

    def on_device(features, memory, requests, owners, labels):
        crops, width = features.shape
        rows = memory.shape[0]
        half = width // 2
        arm = chips // 2
        total = requests.shape[1] * rows
        any_spec = pl.BlockSpec(memory_space=pl.ANY)
        smem = pl.BlockSpec(memory_space=pltpu.SMEM)
        vmem = pl.BlockSpec(memory_space=pltpu.VMEM)
        dma = pltpu.SemaphoreType.DMA
        packed = 2 * max(2, 2 * crops // regions)
        results = pl.pallas_call(
            functools.partial(kernel, chips, side),
            out_shape=(pltpu.VMEM((crops, width), BF16), pltpu.VMEM((rows, width), BF16)),
            in_specs=[any_spec, any_spec, smem, smem, vmem],
            out_specs=(vmem, vmem),
            scratch_shapes=[
                pltpu.VMEM((crops, width), BF16),
                pltpu.VMEM((2, 2 * crops, half), BF16),
                pltpu.VMEM((2, 2, arm - 1, rows, half), BF16),
                pltpu.VMEM((2, 2, 2, packed, half), BF16),
                pltpu.VMEM((2, 2 * packed, half), BF16),
                pltpu.VMEM((2, 4 * packed, half), BF16),
                pltpu.VMEM((2, 1, 2 * crops), jnp.int32),
                pltpu.VMEM((2, arm + 1, 2, 1, 2 * crops), jnp.int32),
                pltpu.VMEM((groups, rows, width), BF16),
                pltpu.VMEM((2, rows, half), BF16),
                pltpu.VMEM((4, rows, half), F32),
                pltpu.VMEM((4, rows, 4 * packed), BF16),
                pltpu.VMEM((rows, crops), F32),
                pltpu.VMEM((total, width), BF16),
                pltpu.VMEM((crops, total), F32),
                pltpu.VMEM((crops, total), BF16),
                pltpu.VMEM((2, rows, half), F32),
                dma((2, 2, arm - 1)),
                dma((2, 2, arm - 1)),
                dma((2, 5)),
                dma((2, 5)),
                dma((2, arm + 1)),
                dma((2, arm + 1)),
                dma((3,)),
                dma((3,)),
                dma((2, 20)),
                dma((2, 20)),
                dma((6,)),
            ],
            compiler_params=pltpu.CompilerParams(
                collective_id=0, has_side_effects=True, vmem_limit_bytes=56 << 20
            ),
        )(features, memory, requests, owners, labels)
        results = [pltpu.with_memory_space_constraint(r, pltpu.VMEM) for r in results]
        return pl.pallas_call(
            hand_over,
            out_shape=(
                jax.ShapeDtypeStruct((crops, width), BF16),
                jax.ShapeDtypeStruct((rows, width), BF16),
            ),
            in_specs=[vmem, vmem],
            out_specs=(any_spec, any_spec),
            scratch_shapes=[dma((2,))],
        )(*results)

    both = P(("region", "group"), None)
    return jax.shard_map(
        on_device,
        mesh=mesh,
        in_specs=(both, both, both, P("region", None), both),
        out_specs=(both, both),
        check_vma=False,
    )
```

```python
import functools

import jax
import jax.numpy as jnp
from jax import lax
from jax.experimental import pallas as pl
from jax.experimental.pallas import tpu as pltpu
from jax.sharding import PartitionSpec as P

MESH = pl.DeviceIdType.MESH
F32 = jnp.float32
BF16 = jnp.bfloat16

SHARPNESS = 0.05
SMOOTHING = 0.1
KEEP = 0.2


def kernel(
    chips, side,
    feat_hbm, mem_hbm, req_hbm, own_hbm, lab_hbm,
    grad, new,
    req_ref, own_ref, lab_ref, feat, halves, ring, packs, near, far, pair, labs, tallies, gath, old, part, move, cand, score, logit, mix,
    ring_send, ring_recv, pack_send, pack_recv, lab_send, lab_recv, tally_send, tally_recv, sib_send, sib_recv, ag_send, ag_recv, last_send, last_recv, loc,
):
    crops, width = feat.shape
    half = width // 2
    rows = old.shape[1]
    packed = near.shape[1] // 2
    slots = packed // 2
    long_arm = chips // 2
    region = lax.axis_index("region")
    group = lax.axis_index("group")
    chip = region // 2
    core = region % 2
    other = 1 - core
    sign = 1 - 2 * core
    gx, gy = group // side, group % side

    def chip_at(offset):
        return (chip + offset + chips) % chips

    def dev(chip_index, core_index, group_index):
        return (chip_index * 2 + core_index, group_index)

    my_cols = pl.ds(pl.multiple_of(core * half, half), half)
    other_cols = pl.ds(pl.multiple_of(other * half, half), half)

    def at_xy(dx, dy):
        return ((gx + dx + side) % side) * side + (gy + dy + side) % side

    partners = [dev(chip, other, group)]
    for step in (1, -1):
        partners.append(dev(chip_at(step), core, group))
        partners.append(dev(chip_at(step), other, group))
        partners.append((region, at_xy(step, 0)))
        partners.append((region, at_xy(0, step)))
    barrier = pltpu.get_barrier_semaphore()
    for partner in partners:
        pl.semaphore_signal(barrier, inc=1, device_id=partner, device_id_type=MESH)

    tables = [
        pltpu.make_async_copy(lab_hbm, lab_ref, loc.at[6]),
        pltpu.make_async_copy(req_hbm, req_ref, loc.at[7]),
        pltpu.make_async_copy(own_hbm, own_ref, loc.at[8]),
    ]
    local = [
        pltpu.make_async_copy(feat_hbm.at[:, my_cols], halves.at[0, pl.ds(0, crops)], loc.at[0]),
        pltpu.make_async_copy(feat_hbm.at[:, other_cols], halves.at[1, pl.ds(0, crops)], loc.at[1]),
        pltpu.make_async_copy(feat_hbm, feat, loc.at[2]),
        pltpu.make_async_copy(mem_hbm.at[:, my_cols], old.at[0], loc.at[3]),
        pltpu.make_async_copy(mem_hbm.at[:, other_cols], old.at[1], loc.at[4]),
        pltpu.make_async_copy(mem_hbm, gath.at[group], loc.at[5]),
    ]
    tables[0].start()
    local[0].start()
    local[1].start()

    before_crop = jnp.where(
        lax.broadcasted_iota(jnp.int32, (crops, crops), 0) < lax.broadcasted_iota(jnp.int32, (crops, crops), 1),
        1.0, 0.0,
    ).astype(BF16)
    tables[0].wait()
    label = lab_ref[...]
    label_region = lax.shift_right_logical(label, jnp.int32(rows.bit_length() - 1))
    of_region = jnp.where(
        lax.broadcasted_iota(jnp.int32, (2 * chips, crops), 0) == label_region, 1.0, 0.0
    )
    earlier = jnp.dot(of_region.astype(BF16), before_crop, preferred_element_type=F32)
    rank = jnp.sum(earlier * of_region, axis=0, keepdims=True).astype(jnp.int32)
    slot_row = label_region * slots + rank
    lanes = pair.shape[2]
    pieces = crops // lanes
    pair[0] = jnp.zeros(pair.shape[1:], jnp.int32)
    for n in range(pieces):
        pair[0, n:n + 1, :] = label[:, n * lanes:(n + 1) * lanes]
        pair[0, pieces + n:pieces + n + 1, :] = slot_row[:, n * lanes:(n + 1) * lanes]

    def row_of(tiles, k, first):
        return jnp.concatenate([tiles[k, first + n:first + n + 1, :] for n in range(pieces)], axis=1)

    def labels_of(tiles, k):
        return row_of(tiles, k, 0)

    def slots_of(tiles, k):
        return row_of(tiles, k, pieces)

    pl.semaphore_wait(barrier, len(partners))

    def remote(src, dst, send, recv, device):
        return pltpu.make_async_remote_copy(
            src_ref=src, dst_ref=dst, send_sem=send, recv_sem=recv, device_id=device, device_id_type=MESH
        )

    sibling = dev(chip, other, group)
    swap = [
        remote(pair.at[0], pair.at[1], sib_send.at[0], sib_recv.at[0], sibling),
        remote(feat_hbm.at[:, other_cols], halves.at[0, pl.ds(crops, crops)], sib_send.at[1], sib_recv.at[1], sibling),
        remote(feat_hbm.at[:, my_cols], halves.at[1, pl.ds(crops, crops)], sib_send.at[2], sib_recv.at[2], sibling),
    ]
    swap[0].start()

    def tile_copy(arm, e):
        towards = sign * (1 - 2 * arm) * (1 - 2 * e)
        return remote(
            pair.at[0], labs.at[arm, 0, e], lab_send.at[arm, e], lab_recv.at[arm, e],
            dev(chip_at(towards), core + e * sign, group),
        )

    def tiles_copy(arm):
        towards = sign * (1 - 2 * arm)
        return remote(
            labs.at[arm, 0], labs.at[arm, 1], lab_send.at[arm, 2], lab_recv.at[arm, 2],
            dev(chip_at(towards), core, group),
        )

    for arm in range(2):
        for e in range(2):
            tile_copy(arm, e).start()

    def pack_copy(stage, arm, e):
        towards = sign * (1 - 2 * arm) * (1 - 2 * e)
        place = pl.ds(pl.multiple_of(e * packed, packed), packed)
        landing = near if stage == 0 else far
        return remote(
            packs.at[stage, arm, e], landing.at[arm, place],
            pack_send.at[arm, 2 * stage + e], pack_recv.at[arm, 2 * stage + e],
            dev(chip_at(towards), core + e * sign, group),
        )

    def forward_copy(arm):
        towards = sign * (1 - 2 * arm)
        return remote(
            near.at[arm], far.at[arm, pl.ds(2 * packed, 2 * packed)], pack_send.at[arm, 4], pack_recv.at[arm, 4],
            dev(chip_at(towards), core, group),
        )

    def send_packed(stage, arm):
        @pl.loop(0, 2)
        def _(e):
            towards = sign * (1 - 2 * arm) * (1 - 2 * e)
            goal = chip_at(towards * (long_arm - arm - stage))
            take = jnp.where(
                lax.broadcasted_iota(jnp.int32, (packed, crops), 0) + goal * packed == slots_of(pair, 0),
                1.0, 0.0,
            ).astype(BF16)
            packs[stage, arm, e] = jnp.dot(
                take, halves[e, 0:crops, :], preferred_element_type=F32
            ).astype(BF16)
            pack_copy(stage, arm, e).start()

    local[0].wait()
    local[1].wait()
    send_packed(0, 0)
    swap[1].start()
    send_packed(1, 0)
    send_packed(0, 1)
    swap[2].start()
    for copy in local[2:] + tables[1:]:
        copy.start()

    offs = (0, -1, 1, 2)

    def block(h, i, j):
        def off(k):
            return k
        dx, dy = (i, j) if h == 0 else (j, i)
        return at_xy(dx, dy)

    def ag_copy(h, index, src_block, rows_of, device_block, own=False):
        cols = pl.ds(h * half, half)
        dst = gath.at[src_block, rows_of, cols]
        src = mem_hbm.at[rows_of, cols] if own else dst
        return remote(src, dst, ag_send.at[h, index], ag_recv.at[h, index], (region, device_block))

    full = pl.ds(0, rows)
    part_of = {1: pl.ds(0, rows // 2), -1: pl.ds(rows // 2, rows // 2)}
    way = {1: 0, -1: 1}

    def p1(h, u, recv=False):
        return ag_copy(h, way[u], block(h, -u, 0) if recv else block(h, 0, 0), full, block(h, u, 0), own=not recv)

    def p2(h, u, recv=False):
        return ag_copy(h, 2 + way[u], block(h, -2 * u if recv else -u, 0), part_of[u], block(h, u, 0))

    def q1(h, a, u, recv=False):
        return ag_copy(
            h, 4 + 2 * a + way[u], block(h, offs[a], -u if recv else 0), full, block(h, 0, u), own=(a == 0 and not recv)
        )

    def q2(h, a, u, recv=False):
        return ag_copy(
            h, 12 + 2 * a + way[u], block(h, offs[a], -2 * u if recv else -u), part_of[u], block(h, 0, u)
        )

    both = (1, -1)

    def gather_round0():
        for u in both:
            for h in range(2):
                p1(h, u).start()
        for u in both:
            for h in range(2):
                q1(h, 0, u).start()

    def gather_round1():
        for h in range(2):
            for u, a in ((1, 1), (-1, 2)):
                p1(h, u, True).wait_recv()
                p2(h, u).start()
                for v in both:
                    q1(h, a, v).start()

    def gather_round1b():
        for h in range(2):
            for u in both:
                q1(h, 0, u, True).wait_recv()
                q2(h, 0, u).start()

    def gather_round2():
        for h in range(2):
            for u in both:
                p2(h, u, True).wait_recv()
            for u in both:
                q1(h, 3, u).start()
        for h in range(2):
            for a in (1, 2):
                for u in both:
                    q1(h, a, u, True).wait_recv()
                    q2(h, a, u).start()

    def gather_round3():
        for h in range(2):
            for u in both:
                q1(h, 3, u, True).wait_recv()
                q2(h, 3, u).start()

    def gather_round4():
        for h in range(2):
            for a in range(4):
                for u in both:
                    q2(h, a, u, True).wait_recv()
        local[5].wait()

    def gather_sent():
        for h in range(2):
            for u in both:
                p1(h, u).wait_send()
                p2(h, u).wait_send()
                for a in range(4):
                    q1(h, a, u).wait_send()
                    q2(h, a, u).wait_send()

    gather_round0()

    places = lax.broadcasted_iota(jnp.int32, (rows, crops), 0)

    def hit(label_row, target):
        return jnp.where(places == label_row - target * rows, 1.0, 0.0)

    def own_pick(target):
        return jnp.concatenate([hit(labels_of(pair, k), target) for k in range(2)], axis=1).astype(BF16)

    def own_sums(pick, which):
        return jnp.dot(pick, halves[which], preferred_element_type=F32)

    def tally(pick):
        ones = jnp.ones((tallies.shape[2], pick.shape[1]), BF16)
        return lax.dot_general(ones, pick, (((1,), (1,)), ((), ())), preferred_element_type=F32)

    def moves(arm, target):
        sources = [(labs.at[arm, hop], k) for hop in range(2) for k in range(2)]
        first = target // 2 * packed
        put, take = [], []
        for n, (source, k) in enumerate(sources):
            slot = slots_of(source, k) - first
            slot = jnp.where((slot >= 0) & (slot < packed), slot + n * packed, -1)
            place = lax.broadcasted_iota(jnp.int32, (4 * packed, crops), 0)
            take.append(jnp.where(place == slot, 1.0, 0.0).astype(BF16))
            put.append(hit(labels_of(source, k), target).astype(BF16))
        put = jnp.concatenate(put, axis=1)
        through = lax.dot_general(
            put, jnp.concatenate(take, axis=1), (((1,), (1,)), ((), ())), preferred_element_type=F32
        )
        return through.astype(BF16), tally(put)

    def ring_copy(t, arm, e, device):
        return remote(
            ring.at[arm, e, t - 2], ring.at[arm, e, t - 1], ring_send.at[arm, e, t - 2], ring_recv.at[arm, e, t - 1],
            device,
        )

    def last_copy(e, r):
        span = pl.ds(r * (rows // 2), rows // 2)
        _, nearest = ring_target(long_arm - 1, 0, e)
        return remote(
            ring.at[0, e, long_arm - 3, span], ring.at[0, e, long_arm - 2, span], last_send.at[e, r], last_recv.at[e, r],
            nearest,
        )

    def ring_target(t, arm, e):
        towards = sign * (1 - 2 * arm)
        distance = long_arm - arm - t
        goal = chip_at(towards * distance) * 2 + core + e * sign
        last = (t + arm) // (long_arm - 1)
        nearest = dev(chip_at(towards), core + last * e * sign, group)
        return goal, nearest

    def tally_copy(t, arm):
        towards = sign * (1 - 2 * arm)
        return remote(
            tallies.at[arm, t - 2], tallies.at[arm, t - 1], tally_send.at[arm, t - 2], tally_recv.at[arm, t - 1],
            dev(chip_at(towards), core, group),
        )

    for arm in range(2):
        for e in range(2):
            tile_copy(arm, e).wait_recv()
        tiles_copy(arm).start()
    swap[0].wait_recv()

    def take_candidates():
        tables[1].wait()
        tables[2].wait()
        for k in range(8):
            cand[k * rows:(k + 1) * rows, :] = gath[own_ref[0, req_ref[0, k]]]

    def scores():
        local[2].wait()

        @pl.loop(0, 4)
        def _(n):
            span = pl.ds(pl.multiple_of(n * 256, 256), 256)
            score[:, span] = lax.dot_general(
                feat[...], cand[span, :], (((1,), (1,)), ((), ())), preferred_element_type=F32
            ) * (1.0 / SHARPNESS)

    def softmax():
        total = cand.shape[0]

        @pl.loop(0, crops // 64)
        def _(n):
            span = pl.ds(pl.multiple_of(n * 64, 64), 64)
            s = score[span, :]
            expo = jnp.exp(s - jnp.max(s, axis=1, keepdims=True))
            prob = expo / jnp.sum(expo, axis=1, keepdims=True)
            column = lax.broadcasted_iota(jnp.int32, s.shape, 1)
            target = jnp.where(column < rows, (1.0 - SMOOTHING) / rows, 0.0) + SMOOTHING / total
            logit[span, :] = ((prob - target) * (1.0 / SHARPNESS)).astype(BF16)

    def grads():
        @pl.loop(0, width // 256)
        def _(n):
            span = pl.ds(pl.multiple_of(n * 256, 256), 256)
            grad[:, span] = jnp.dot(logit[...], cand[:, span], preferred_element_type=F32).astype(BF16)

    for arm in range(2):
        for e in range(2):
            pack_copy(0, arm, e).wait_recv()
        forward_copy(arm).start()
        if arm == 0:
            send_packed(1, 1)
    swap[1].wait_recv()

    for arm in range(2):
        @pl.loop(0, 2)
        def _(e):
            goal, _ = ring_target(2, arm, e)
            part[2 * arm + e] = own_sums(own_pick(goal), 0)

        if arm == 0:
            gather_round1()
        tiles_copy(arm).wait_recv()

        @pl.loop(0, 2)
        def _(e):
            goal, _ = ring_target(2, arm, e)
            through, number = moves(arm, goal)
            move[2 * arm + e] = through

            @pl.when(e == 0)
            def _():
                tallies[arm, 0] = number + tally(own_pick(goal))
                tally_copy(2, arm).start()

        for e in range(2):
            pack_copy(1, arm, e).wait_recv()
        forward_copy(arm).wait_recv()

        @pl.loop(0, 2)
        def _(e):
            _, nearest = ring_target(2, arm, e)
            come = jnp.dot(move[2 * arm + e], far[arm], preferred_element_type=F32)
            ring[arm, e, 0] = (part[2 * arm + e] + come).astype(BF16)
            ring_copy(2, arm, e, nearest).start()

    gather_round1b()

    @pl.loop(3, long_arm - 1)
    def _(t):
        @pl.loop(0, 4)
        def _(q):
            arm, e = q // 2, q % 2
            goal, nearest = ring_target(t, arm, e)
            pick = own_pick(goal)
            part[0] = own_sums(pick, 0)

            @pl.when(e == 0)
            def _():
                number = tally(pick)
                tally_copy(t - 1, arm).wait_recv()
                tallies[arm, t - 2] = tallies[arm, t - 2] + number
                tally_copy(t, arm).start()

            ring_copy(t - 1, arm, e, nearest).wait_recv()
            ring[arm, e, t - 2] = (part[0] + ring[arm, e, t - 2].astype(F32)).astype(BF16)
            ring_copy(t, arm, e, nearest).start()

        @pl.when(t == 3)
        def _():
            gather_round2()

        @pl.when(t == 4)
        def _():
            gather_round3()

        @pl.when(t == 5)
        def _():
            gather_round4()
            take_candidates()
            scores()

        @pl.when(t == 6)
        def _():
            softmax()
            grads()

    for e in range(2):
        goal, _ = ring_target(long_arm - 1, 0, e)
        pick = own_pick(goal)
        part[0] = own_sums(pick, 0)
        if e == 0:
            number = tally(pick)
            tally_copy(long_arm - 2, 0).wait_recv()
            tallies[0, long_arm - 3] = tallies[0, long_arm - 3] + number
            tally_copy(long_arm - 1, 0).start()
        ring_copy(long_arm - 2, 0, e, sibling).wait_recv()
        for r in range(2):
            span = pl.ds(r * (rows // 2), rows // 2)
            ring[0, e, long_arm - 3, span, :] = (
                part[0, span, :] + ring[0, e, long_arm - 3, span, :].astype(F32)
            ).astype(BF16)
            last_copy(e, r).start()

    pick = own_pick(region)
    tally_copy(long_arm - 2, 1).wait_recv()
    tally_copy(long_arm - 1, 0).wait_recv()
    number = tally(pick) + tallies[0, long_arm - 2] + tallies[1, long_arm - 3]
    square_of = (rows, rows)
    diagonal = lax.broadcasted_iota(jnp.int32, square_of, 0) == lax.broadcasted_iota(jnp.int32, square_of, 1)
    counts = jnp.sum(jnp.where(diagonal, number[0:1, :], 0.0), axis=1, keepdims=True)
    keep = jnp.where(counts > 0, KEEP, 1.0)
    take = jnp.where(counts > 0, (1.0 - KEEP) / jnp.maximum(counts, 1.0), 0.0)
    swap[2].wait_recv()
    local[3].wait()
    local[4].wait()
    for which in range(2):
        part[0] = own_sums(pick, which)
        ring_copy(long_arm - 2, 1, which, sibling).wait_recv()
        mix[which] = keep * old[which].astype(F32) + take * (part[0] + ring[1, which, long_arm - 3].astype(F32))
    square = [None, None]
    for which, cols in ((0, my_cols), (1, other_cols)):
        for r in range(2):
            span = pl.ds(r * (rows // 2), rows // 2)
            last_copy(which, r).wait_recv()
            mixed = mix[which, span, :] + take[r * (rows // 2):(r + 1) * (rows // 2)] * ring[
                0, which, long_arm - 2, span, :
            ].astype(F32)
            ones = jnp.sum(mixed * mixed, axis=1, keepdims=True)
            if which == 0:
                mix[0, span, :] = mixed
                square[r] = ones
            else:
                scale = lax.rsqrt((square[r] + ones) * (1.0 / width) + 1e-06) * width ** (-0.5)
                new[span, cols] = (mixed * scale).astype(BF16)
                new[span, my_cols] = (mix[0, span, :] * scale).astype(BF16)

    for copy in swap:
        copy.wait_send()
    gather_sent()
    for arm in range(2):
        forward_copy(arm).wait_send()
        for e in range(2):
            for stage in range(2):
                pack_copy(stage, arm, e).wait_send()

        tiles_copy(arm).wait_send()
        for e in range(2):
            tile_copy(arm, e).wait_send()

        @pl.loop(2, long_arm - 1)
        def _(t):
            tally_copy(t, arm).wait_send()
            for e in range(2):
                ring_copy(t, arm, e, sibling).wait_send()
    tally_copy(long_arm - 1, 0).wait_send()
    for e in range(2):
        for r in range(2):
            last_copy(e, r).wait_send()


def hand_over(grad, new, grad_out, new_out, sem):
    copies = [
        pltpu.make_async_copy(grad, grad_out, sem.at[0]),
        pltpu.make_async_copy(new, new_out, sem.at[1]),
    ]
    for copy in copies:
        copy.start()
    for copy in copies:
        copy.wait()


def solution(mesh):
    regions, groups = mesh.shape["region"], mesh.shape["group"]
    chips = regions // 2
    side = int(round(groups ** 0.5))

    def on_device(features, memory, requests, owners, labels):
        crops, width = features.shape
        rows = memory.shape[0]
        half = width // 2
        arm = chips // 2
        total = requests.shape[1] * rows
        any_spec = pl.BlockSpec(memory_space=pl.ANY)
        vmem = pl.BlockSpec(memory_space=pltpu.VMEM)
        dma = pltpu.SemaphoreType.DMA
        packed = 2 * max(2, 2 * crops // regions)
        results = pl.pallas_call(
            functools.partial(kernel, chips, side),
            out_shape=(pltpu.VMEM((crops, width), BF16), pltpu.VMEM((rows, width), BF16)),
            in_specs=[any_spec] * 5,
            out_specs=(vmem, vmem),
            scratch_shapes=[
                pltpu.SMEM(requests.shape, jnp.int32),
                pltpu.SMEM(owners.shape, jnp.int32),
                pltpu.VMEM(labels.shape, jnp.int32),
                pltpu.VMEM((crops, width), BF16),
                pltpu.VMEM((2, 2 * crops, half), BF16),
                pltpu.VMEM((2, 2, arm - 1, rows, half), BF16),
                pltpu.VMEM((2, 2, 2, packed, half), BF16),
                pltpu.VMEM((2, 2 * packed, half), BF16),
                pltpu.VMEM((2, 4 * packed, half), BF16),
                pltpu.VMEM((2, 8, 128), jnp.int32),
                pltpu.VMEM((2, 2, 2, 8, 128), jnp.int32),
                pltpu.VMEM((2, arm - 1, 8, 128), F32),
                pltpu.VMEM((groups, rows, width), BF16),
                pltpu.VMEM((2, rows, half), BF16),
                pltpu.VMEM((4, rows, half), F32),
                pltpu.VMEM((4, rows, 4 * packed), BF16),
                pltpu.VMEM((total, width), BF16),
                pltpu.VMEM((crops, total), F32),
                pltpu.VMEM((crops, total), BF16),
                pltpu.VMEM((2, rows, half), F32),
                dma((2, 2, arm - 1)),
                dma((2, 2, arm - 1)),
                dma((2, 5)),
                dma((2, 5)),
                dma((2, 3)),
                dma((2, 3)),
                dma((2, arm - 1)),
                dma((2, arm - 1)),
                dma((3,)),
                dma((3,)),
                dma((2, 20)),
                dma((2, 20)),
                dma((2, 2)),
                dma((2, 2)),
                dma((9,)),
            ],
            compiler_params=pltpu.CompilerParams(
                collective_id=0, has_side_effects=True, vmem_limit_bytes=56 << 20
            ),
        )(features, memory, requests, owners, labels)
        results = [pltpu.with_memory_space_constraint(r, pltpu.VMEM) for r in results]
        return pl.pallas_call(
            hand_over,
            out_shape=(
                jax.ShapeDtypeStruct((crops, width), BF16),
                jax.ShapeDtypeStruct((rows, width), BF16),
            ),
            in_specs=[vmem, vmem],
            out_specs=(any_spec, any_spec),
            scratch_shapes=[dma((2,))],
        )(*results)

    both = P(("region", "group"), None)
    return jax.shard_map(
        on_device,
        mesh=mesh,
        in_specs=(both, both, both, P("region", None), both),
        out_specs=(both, both),
        check_vma=False,
    )
```

```python
import functools

import jax
import jax.numpy as jnp
from jax import lax
from jax.experimental import pallas as pl
from jax.experimental.pallas import tpu as pltpu
from jax.sharding import PartitionSpec as P

MESH = pl.DeviceIdType.MESH
F32 = jnp.float32
BF16 = jnp.bfloat16

SHARPNESS = 0.05
SMOOTHING = 0.1
KEEP = 0.2


def kernel(
    chips, side,
    feat_hbm, mem_hbm, req_hbm, own_hbm, lab_hbm,
    grad, new,
    req_ref, own_ref, lab_ref, feat, halves, ring, packs, near, far, pair, labs, tallies, gath, old, part, move, cand, score, logit, mix,
    ring_send, ring_recv, pack_send, pack_recv, lab_send, lab_recv, tally_send, tally_recv, sib_send, sib_recv, ag_send, ag_recv, last_recv, loc,
):
    crops, width = feat.shape
    half = width // 2
    rows = old.shape[1]
    packed = near.shape[1] // 2
    slots = packed // 2
    long_arm = chips // 2
    region = lax.axis_index("region")
    group = lax.axis_index("group")
    chip = region // 2
    core = region % 2
    other = 1 - core
    sign = 1 - 2 * core
    gx, gy = group // side, group % side

    def chip_at(offset):
        return (chip + offset + chips) % chips

    def dev(chip_index, core_index, group_index):
        return (chip_index * 2 + core_index, group_index)

    my_cols = pl.ds(pl.multiple_of(core * half, half), half)
    other_cols = pl.ds(pl.multiple_of(other * half, half), half)

    def at_xy(dx, dy):
        return ((gx + dx + side) % side) * side + (gy + dy + side) % side

    partners = [dev(chip, other, group)]
    for step in (1, -1):
        partners.append(dev(chip_at(step), core, group))
        partners.append(dev(chip_at(step), other, group))
        partners.append((region, at_xy(step, 0)))
        partners.append((region, at_xy(0, step)))
    barrier = pltpu.get_barrier_semaphore()
    for partner in partners:
        pl.semaphore_signal(barrier, inc=1, device_id=partner, device_id_type=MESH)

    tables = [
        pltpu.make_async_copy(lab_hbm, lab_ref, loc.at[6]),
        pltpu.make_async_copy(req_hbm, req_ref, loc.at[7]),
        pltpu.make_async_copy(own_hbm, own_ref, loc.at[8]),
    ]
    local = [
        pltpu.make_async_copy(feat_hbm.at[:, my_cols], halves.at[0, pl.ds(0, crops)], loc.at[0]),
        pltpu.make_async_copy(feat_hbm.at[:, other_cols], halves.at[1, pl.ds(0, crops)], loc.at[1]),
        pltpu.make_async_copy(feat_hbm, feat, loc.at[2]),
        pltpu.make_async_copy(mem_hbm.at[:, my_cols], old.at[0], loc.at[3]),
        pltpu.make_async_copy(mem_hbm.at[:, other_cols], old.at[1], loc.at[4]),
        pltpu.make_async_copy(mem_hbm, gath.at[group], loc.at[5]),
    ]
    tables[0].start()
    local[0].start()
    local[1].start()

    lanes = pair.shape[2]
    pieces = crops // lanes
    square_of = (lanes, lanes)
    sooner = jnp.where(
        lax.broadcasted_iota(jnp.int32, square_of, 0) < lax.broadcasted_iota(jnp.int32, square_of, 1), 1.0, 0.0
    ).astype(BF16)
    pair[0] = jnp.zeros(pair.shape[1:], jnp.int32)
    region_of = lax.broadcasted_iota(jnp.int32, (2 * chips, lanes), 0)
    tables[0].wait()
    split = [lab_ref[:, n * lanes:(n + 1) * lanes] for n in range(pieces)]
    homes = [lax.shift_right_logical(piece, jnp.int32(rows.bit_length() - 1)) for piece in split]
    of_region = [jnp.where(region_of == home, 1.0, 0.0) for home in homes]
    earlier = jnp.dot(
        jnp.concatenate(of_region, axis=0).astype(BF16), sooner, preferred_element_type=F32
    )
    seen = jnp.zeros((2 * chips, 1), F32)
    for n in range(pieces):
        rank = jnp.sum(
            (earlier[n * 2 * chips:(n + 1) * 2 * chips] + seen) * of_region[n], axis=0, keepdims=True
        ).astype(jnp.int32)
        seen += jnp.sum(of_region[n], axis=1, keepdims=True)
        pair[0, n:n + 1, :] = split[n]
        pair[0, pieces + n:pieces + n + 1, :] = homes[n] * slots + rank

    def row_of(tiles, k, first):
        return jnp.concatenate([tiles[k, first + n:first + n + 1, :] for n in range(pieces)], axis=1)

    def labels_of(tiles, k):
        return row_of(tiles, k, 0)

    def slots_of(tiles, k):
        return row_of(tiles, k, pieces)

    pl.semaphore_wait(barrier, len(partners))

    def remote(src, dst, send, recv, device):
        return pltpu.make_async_remote_copy(
            src_ref=src, dst_ref=dst, send_sem=send, recv_sem=recv, device_id=device, device_id_type=MESH
        )

    sibling = dev(chip, other, group)
    swap = [
        remote(pair.at[0], pair.at[1], sib_send.at[0], sib_recv.at[0], sibling),
        remote(feat_hbm.at[:, other_cols], halves.at[0, pl.ds(crops, crops)], sib_send.at[1], sib_recv.at[1], sibling),
        remote(feat_hbm.at[:, my_cols], halves.at[1, pl.ds(crops, crops)], sib_send.at[1], sib_recv.at[2], sibling),
    ]
    swap[0].start()

    def tile_copy(arm, e):
        towards = sign * (1 - 2 * arm) * (1 - 2 * e)
        return remote(
            pair.at[0], labs.at[arm, 0, e], lab_send.at[0], lab_recv.at[arm, 0],
            dev(chip_at(towards), core + e * sign, group),
        )

    def tiles_copy(arm):
        towards = sign * (1 - 2 * arm)
        return remote(
            labs.at[arm, 0], labs.at[arm, 1], lab_send.at[0], lab_recv.at[arm, 1],
            dev(chip_at(towards), core, group),
        )

    for arm in range(2):
        for e in range(2):
            tile_copy(arm, e).start()

    def pack_copy(stage, arm, e):
        towards = sign * (1 - 2 * arm) * (1 - 2 * e)
        place = pl.ds(pl.multiple_of(e * packed, packed), packed)
        landing = near if stage == 0 else far
        return remote(
            packs.at[stage, arm, e], landing.at[arm, place],
            pack_send.at[0], pack_recv.at[arm, stage],
            dev(chip_at(towards), core + e * sign, group),
        )

    def forward_copy(arm):
        towards = sign * (1 - 2 * arm)
        return remote(
            near.at[arm], far.at[arm, pl.ds(2 * packed, 2 * packed)], pack_send.at[1], pack_recv.at[arm, 1],
            dev(chip_at(towards), core, group),
        )

    def packs_here(arm, stage):
        landing = (near if stage == 0 else far).at[arm]
        return remote(landing, landing, pack_send.at[0], pack_recv.at[arm, stage], sibling)

    def send_packed(stage, arm):
        @pl.loop(0, 2)
        def _(e):
            towards = sign * (1 - 2 * arm) * (1 - 2 * e)
            goal = chip_at(towards * (long_arm - arm - stage))
            take = jnp.where(
                lax.broadcasted_iota(jnp.int32, (packed, crops), 0) + goal * packed == slots_of(pair, 0),
                1.0, 0.0,
            ).astype(BF16)
            packs[stage, arm, e] = jnp.dot(
                take, halves[e, 0:crops, :], preferred_element_type=F32
            ).astype(BF16)
            pack_copy(stage, arm, e).start()

    local[0].wait()
    local[1].wait()
    send_packed(0, 0)
    swap[1].start()
    send_packed(1, 0)
    send_packed(0, 1)
    swap[2].start()
    for copy in local[2:] + tables[1:]:
        copy.start()

    offs = (0, -1, 1, 2)

    def block(h, i, j):
        def off(k):
            return k
        dx, dy = (i, j) if h == 0 else (j, i)
        return at_xy(dx, dy)

    def ag_copy(h, kind, src_block, rows_of, device_block, own=False):
        cols = pl.ds(h * half, half)
        dst = gath.at[src_block, rows_of, cols]
        src = mem_hbm.at[rows_of, cols] if own else dst
        return remote(src, dst, ag_send.at[kind], ag_recv.at[kind], (region, device_block))

    full = pl.ds(0, rows)
    part_of = {1: pl.ds(0, rows // 2), -1: pl.ds(rows // 2, rows // 2)}

    def p1(h, u, recv=False):
        return ag_copy(h, 0, block(h, -u, 0) if recv else block(h, 0, 0), full, block(h, u, 0), own=not recv)

    def p2(h, u, recv=False):
        return ag_copy(h, 1, block(h, -2 * u if recv else -u, 0), part_of[u], block(h, u, 0))

    def q1(h, a, u, recv=False):
        return ag_copy(
            h, (2, 3, 3, 4)[a], block(h, offs[a], -u if recv else 0), full, block(h, 0, u), own=(a == 0 and not recv)
        )

    def q2(h, a, u, recv=False):
        return ag_copy(
            h, 5, block(h, offs[a], -2 * u if recv else -u), part_of[u], block(h, 0, u)
        )

    both = (1, -1)

    def gather_round0():
        for u in both:
            for h in range(2):
                p1(h, u).start()
        for u in both:
            for h in range(2):
                q1(h, 0, u).start()

    amounts = (2, 1, 2, 4, 2, 4)

    def whole(kind):
        some = gath.at[pl.ds(0, amounts[kind])]
        return remote(some, some, ag_send.at[kind], ag_recv.at[kind], sibling)

    def gather_round1():
        whole(0).wait_recv()
        for h in range(2):
            for u, a in ((1, 1), (-1, 2)):
                p2(h, u).start()
                for v in both:
                    q1(h, a, v).start()

    def gather_round1b():
        whole(2).wait_recv()
        for h in range(2):
            for u in both:
                q2(h, 0, u).start()

    def gather_round2():
        whole(1).wait_recv()
        for h in range(2):
            for u in both:
                q1(h, 3, u).start()
        whole(3).wait_recv()
        for h in range(2):
            for a in (1, 2):
                for u in both:
                    q2(h, a, u).start()

    def gather_round3():
        whole(4).wait_recv()
        for h in range(2):
            for u in both:
                q2(h, 3, u).start()

    def gather_round4():
        whole(5).wait_recv()
        local[5].wait()

    def gather_sent():
        for kind in range(len(amounts)):
            whole(kind).wait_send()

    gather_round0()

    places = lax.broadcasted_iota(jnp.int32, (rows, crops), 0)

    def hit(label_row, target):
        return jnp.where(places == label_row - target * rows, 1.0, 0.0)

    def own_pick(target):
        return jnp.concatenate([hit(labels_of(pair, k), target) for k in range(2)], axis=1).astype(BF16)

    def own_sums(pick, which):
        return jnp.dot(pick, halves[which], preferred_element_type=F32)

    def tally(pick):
        ones = jnp.ones((tallies.shape[2], pick.shape[1]), BF16)
        return lax.dot_general(ones, pick, (((1,), (1,)), ((), ())), preferred_element_type=F32)

    def moves(arm, target):
        sources = [(labs.at[arm, hop], k) for hop in range(2) for k in range(2)]
        first = target // 2 * packed
        put, take = [], []
        for n, (source, k) in enumerate(sources):
            slot = slots_of(source, k) - first
            slot = jnp.where((slot >= 0) & (slot < packed), slot + n * packed, -1)
            place = lax.broadcasted_iota(jnp.int32, (4 * packed, crops), 0)
            take.append(jnp.where(place == slot, 1.0, 0.0).astype(BF16))
            put.append(hit(labels_of(source, k), target).astype(BF16))
        put = jnp.concatenate(put, axis=1)
        through = lax.dot_general(
            put, jnp.concatenate(take, axis=1), (((1,), (1,)), ((), ())), preferred_element_type=F32
        )
        return through.astype(BF16), tally(put)

    def ring_copy(t, arm, e, device):
        return remote(
            ring.at[arm, e, t - 2], ring.at[arm, e, t - 1], ring_send.at[arm], ring_recv.at[arm, e, t - 2],
            device,
        )

    def last_copy(e, r):
        span = pl.ds(r * (rows // 2), rows // 2)
        _, nearest = ring_target(long_arm - 1, 0, e)
        return remote(
            ring.at[0, e, long_arm - 3, span], ring.at[0, e, long_arm - 2, span], ring_send.at[0], last_recv.at[e, r],
            nearest,
        )

    def ring_target(t, arm, e):
        towards = sign * (1 - 2 * arm)
        distance = long_arm - arm - t
        goal = chip_at(towards * distance) * 2 + core + e * sign
        last = (t + arm) // (long_arm - 1)
        nearest = dev(chip_at(towards), core + last * e * sign, group)
        return goal, nearest

    def tally_copy(t, arm):
        towards = sign * (1 - 2 * arm)
        return remote(
            tallies.at[arm, t - 2], tallies.at[arm, t - 1], tally_send.at[arm], tally_recv.at[arm, t - 2],
            dev(chip_at(towards), core, group),
        )

    for arm in range(2):
        remote(pair, labs.at[arm, 0], lab_send.at[0], lab_recv.at[arm, 0], sibling).wait_recv()
        tiles_copy(arm).start()
    swap[0].wait_recv()

    def take_candidates():
        tables[1].wait()
        tables[2].wait()
        for k in range(8):
            cand[k * rows:(k + 1) * rows, :] = gath[own_ref[0, req_ref[0, k]]]

    def scores():
        local[2].wait()

        @pl.loop(0, 4)
        def _(n):
            span = pl.ds(pl.multiple_of(n * 256, 256), 256)
            score[:, span] = lax.dot_general(
                feat[...], cand[span, :], (((1,), (1,)), ((), ())), preferred_element_type=F32
            ) * (1.0 / SHARPNESS)

    def softmax():
        total = cand.shape[0]

        @pl.loop(0, crops // 64)
        def _(n):
            span = pl.ds(pl.multiple_of(n * 64, 64), 64)
            s = score[span, :]
            expo = jnp.exp(s - jnp.max(s, axis=1, keepdims=True))
            prob = expo / jnp.sum(expo, axis=1, keepdims=True)
            column = lax.broadcasted_iota(jnp.int32, s.shape, 1)
            target = jnp.where(column < rows, (1.0 - SMOOTHING) / rows, 0.0) + SMOOTHING / total
            logit[span, :] = ((prob - target) * (1.0 / SHARPNESS)).astype(BF16)

    def grads():
        @pl.loop(0, width // 256)
        def _(n):
            span = pl.ds(pl.multiple_of(n * 256, 256), 256)
            grad[:, span] = jnp.dot(logit[...], cand[:, span], preferred_element_type=F32).astype(BF16)

    for arm in range(2):
        packs_here(arm, 0).wait_recv()
        forward_copy(arm).start()
        if arm == 0:
            send_packed(1, 1)
    swap[1].wait_recv()

    for arm in range(2):
        @pl.loop(0, 2)
        def _(e):
            goal, _ = ring_target(2, arm, e)
            part[2 * arm + e] = own_sums(own_pick(goal), 0)

        if arm == 0:
            gather_round1()
        tiles_copy(arm).wait_recv()

        @pl.loop(0, 2)
        def _(e):
            goal, _ = ring_target(2, arm, e)
            through, number = moves(arm, goal)
            move[2 * arm + e] = through

            @pl.when(e == 0)
            def _():
                tallies[arm, 0] = number + tally(own_pick(goal))
                tally_copy(2, arm).start()

        packs_here(arm, 1).wait_recv()

        @pl.loop(0, 2)
        def _(e):
            _, nearest = ring_target(2, arm, e)
            come = jnp.dot(move[2 * arm + e], far[arm], preferred_element_type=F32)
            ring[arm, e, 0] = (part[2 * arm + e] + come).astype(BF16)
            ring_copy(2, arm, e, nearest).start()

    gather_round1b()

    @pl.loop(3, long_arm - 1)
    def _(t):
        @pl.loop(0, 4)
        def _(q):
            arm, e = q // 2, q % 2
            goal, nearest = ring_target(t, arm, e)
            pick = own_pick(goal)
            part[0] = own_sums(pick, 0)

            @pl.when(e == 0)
            def _():
                number = tally(pick)
                tally_copy(t - 1, arm).wait_recv()
                tallies[arm, t - 2] = tallies[arm, t - 2] + number
                tally_copy(t, arm).start()

            ring_copy(t - 1, arm, e, nearest).wait_recv()
            ring[arm, e, t - 2] = (part[0] + ring[arm, e, t - 2].astype(F32)).astype(BF16)
            ring_copy(t, arm, e, nearest).start()

        @pl.when(t == 3)
        def _():
            gather_round2()

        @pl.when(t == 4)
        def _():
            gather_round3()

        @pl.when(t == 5)
        def _():
            gather_round4()
            take_candidates()
            scores()

        @pl.when(t == 6)
        def _():
            softmax()
            grads()

    for e in range(2):
        goal, _ = ring_target(long_arm - 1, 0, e)
        pick = own_pick(goal)
        part[0] = own_sums(pick, 0)
        if e == 0:
            number = tally(pick)
            tally_copy(long_arm - 2, 0).wait_recv()
            tallies[0, long_arm - 3] = tallies[0, long_arm - 3] + number
            tally_copy(long_arm - 1, 0).start()
        ring_copy(long_arm - 2, 0, e, sibling).wait_recv()
        for r in range(2):
            span = pl.ds(r * (rows // 2), rows // 2)
            ring[0, e, long_arm - 3, span, :] = (
                part[0, span, :] + ring[0, e, long_arm - 3, span, :].astype(F32)
            ).astype(BF16)
            last_copy(e, r).start()

    pick = own_pick(region)
    tally_copy(long_arm - 2, 1).wait_recv()
    tally_copy(long_arm - 1, 0).wait_recv()
    number = tally(pick) + tallies[0, long_arm - 2] + tallies[1, long_arm - 3]
    own_place = (rows, rows)
    diagonal = lax.broadcasted_iota(jnp.int32, own_place, 0) == lax.broadcasted_iota(jnp.int32, own_place, 1)
    counts = jnp.sum(jnp.where(diagonal, number[0:1, :], 0.0), axis=1, keepdims=True)
    keep = jnp.where(counts > 0, KEEP, 1.0)
    take = jnp.where(counts > 0, (1.0 - KEEP) / jnp.maximum(counts, 1.0), 0.0)
    swap[2].wait_recv()
    local[3].wait()
    local[4].wait()
    for which in range(2):
        part[0] = own_sums(pick, which)
        ring_copy(long_arm - 2, 1, which, sibling).wait_recv()
        mix[which] = keep * old[which].astype(F32) + take * (part[0] + ring[1, which, long_arm - 3].astype(F32))
    swap[0].wait_send()
    remote(halves.at[0], halves.at[0], sib_send.at[1], sib_recv.at[1], sibling).wait_send()
    gather_sent()
    remote(packs, packs, pack_send.at[0], pack_recv.at[0, 0], sibling).wait_send()
    remote(near, near, pack_send.at[1], pack_recv.at[0, 0], sibling).wait_send()
    remote(labs, labs, lab_send.at[0], lab_recv.at[0, 0], sibling).wait_send()
    square = [None, None]
    for which, cols in ((0, my_cols), (1, other_cols)):
        for r in range(2):
            span = pl.ds(r * (rows // 2), rows // 2)
            last_copy(which, r).wait_recv()
            mixed = mix[which, span, :] + take[r * (rows // 2):(r + 1) * (rows // 2)] * ring[
                0, which, long_arm - 2, span, :
            ].astype(F32)
            ones = jnp.sum(mixed * mixed, axis=1, keepdims=True)
            if which == 0:
                mix[0, span, :] = mixed
                square[r] = ones
            else:
                scale = lax.rsqrt((square[r] + ones) * (1.0 / width) + 1e-06) * width ** (-0.5)
                new[span, cols] = (mixed * scale).astype(BF16)
                new[span, my_cols] = (mix[0, span, :] * scale).astype(BF16)

    for arm in range(2):
        sent = tallies.at[arm, pl.ds(0, long_arm - 2 - arm)]
        remote(sent, sent, tally_send.at[arm], tally_recv.at[arm, 0], sibling).wait_send()
        sent = ring.at[arm, :, pl.ds(0, long_arm - 2 - arm)]
        remote(sent, sent, ring_send.at[arm], ring_recv.at[arm, 0, 0], sibling).wait_send()


def hand_over(grad, new, grad_out, new_out, sem):
    copies = [
        pltpu.make_async_copy(grad, grad_out, sem.at[0]),
        pltpu.make_async_copy(new, new_out, sem.at[1]),
    ]
    for copy in copies:
        copy.start()
    for copy in copies:
        copy.wait()


def solution(mesh):
    regions, groups = mesh.shape["region"], mesh.shape["group"]
    chips = regions // 2
    side = int(round(groups ** 0.5))

    def on_device(features, memory, requests, owners, labels):
        crops, width = features.shape
        rows = memory.shape[0]
        half = width // 2
        arm = chips // 2
        total = requests.shape[1] * rows
        any_spec = pl.BlockSpec(memory_space=pl.ANY)
        vmem = pl.BlockSpec(memory_space=pltpu.VMEM)
        dma = pltpu.SemaphoreType.DMA
        packed = 2 * max(2, 2 * crops // regions)
        results = pl.pallas_call(
            functools.partial(kernel, chips, side),
            out_shape=(pltpu.VMEM((crops, width), BF16), pltpu.VMEM((rows, width), BF16)),
            in_specs=[any_spec] * 5,
            out_specs=(vmem, vmem),
            scratch_shapes=[
                pltpu.SMEM(requests.shape, jnp.int32),
                pltpu.SMEM(owners.shape, jnp.int32),
                pltpu.VMEM(labels.shape, jnp.int32),
                pltpu.VMEM((crops, width), BF16),
                pltpu.VMEM((2, 2 * crops, half), BF16),
                pltpu.VMEM((2, 2, arm - 1, rows, half), BF16),
                pltpu.VMEM((2, 2, 2, packed, half), BF16),
                pltpu.VMEM((2, 2 * packed, half), BF16),
                pltpu.VMEM((2, 4 * packed, half), BF16),
                pltpu.VMEM((2, 8, 128), jnp.int32),
                pltpu.VMEM((2, 2, 2, 8, 128), jnp.int32),
                pltpu.VMEM((2, arm - 1, 8, 128), F32),
                pltpu.VMEM((groups, rows, width), BF16),
                pltpu.VMEM((2, rows, half), BF16),
                pltpu.VMEM((4, rows, half), F32),
                pltpu.VMEM((4, rows, 4 * packed), BF16),
                pltpu.VMEM((total, width), BF16),
                pltpu.VMEM((crops, total), F32),
                pltpu.VMEM((crops, total), BF16),
                pltpu.VMEM((2, rows, half), F32),
                dma((2,)),
                dma((2, 2, arm - 3)),
                dma((2,)),
                dma((2, 2)),
                dma((1,)),
                dma((2, 2)),
                dma((2,)),
                dma((2, arm - 2)),
                dma((2,)),
                dma((3,)),
                dma((6,)),
                dma((6,)),
                dma((2, 2)),
                dma((9,)),
            ],
            compiler_params=pltpu.CompilerParams(
                collective_id=0, has_side_effects=True, vmem_limit_bytes=56 << 20
            ),
        )(features, memory, requests, owners, labels)
        results = [pltpu.with_memory_space_constraint(r, pltpu.VMEM) for r in results]
        return pl.pallas_call(
            hand_over,
            out_shape=(
                jax.ShapeDtypeStruct((crops, width), BF16),
                jax.ShapeDtypeStruct((rows, width), BF16),
            ),
            in_specs=[vmem, vmem],
            out_specs=(any_spec, any_spec),
            scratch_shapes=[dma((2,))],
        )(*results)

    both = P(("region", "group"), None)
    return jax.shard_map(
        on_device,
        mesh=mesh,
        in_specs=(both, both, both, P("region", None), both),
        out_specs=(both, both),
        check_vma=False,
    )
```

```python
import functools

import jax
import jax.numpy as jnp
from jax import lax
from jax.experimental import pallas as pl
from jax.experimental.pallas import tpu as pltpu
from jax.sharding import PartitionSpec as P

MESH = pl.DeviceIdType.MESH
F32 = jnp.float32
BF16 = jnp.bfloat16

SHARPNESS = 0.05
SMOOTHING = 0.1
KEEP = 0.2


def kernel(
    chips, side,
    feat_hbm, mem_hbm, req_hbm, own_hbm, lab_hbm,
    grad, new,
    req_ref, own_ref, lab_ref, feat, halves, ring, packs, near, far, pair, labs, tallies, gath, old, part, move, cand, score, logit, mix,
    ring_send, ring_recv, pack_send, pack_recv, lab_send, lab_recv, tally_send, tally_recv, sib_send, sib_recv, ag_send, ag_recv, last_recv, loc,
):
    crops, width = feat.shape
    half = width // 2
    rows = old.shape[1]
    packed = near.shape[1] // 2
    slots = packed // 2
    long_arm = chips // 2
    region = lax.axis_index("region")
    group = lax.axis_index("group")
    chip = region // 2
    core = region % 2
    other = 1 - core
    sign = 1 - 2 * core
    gx, gy = group // side, group % side

    def chip_at(offset):
        return (chip + offset + chips) % chips

    def dev(chip_index, core_index, group_index):
        return (chip_index * 2 + core_index, group_index)

    my_cols = pl.ds(pl.multiple_of(core * half, half), half)
    other_cols = pl.ds(pl.multiple_of(other * half, half), half)

    def at_xy(dx, dy):
        return ((gx + dx + side) % side) * side + (gy + dy + side) % side

    partners = [dev(chip, other, group)]
    for step in (1, -1):
        partners.append(dev(chip_at(step), core, group))
        partners.append(dev(chip_at(step), other, group))
        partners.append((region, at_xy(step, 0)))
        partners.append((region, at_xy(0, step)))
    barrier = pltpu.get_barrier_semaphore()
    for partner in partners:
        pl.semaphore_signal(barrier, inc=1, device_id=partner, device_id_type=MESH)

    tables = [
        pltpu.make_async_copy(lab_hbm, lab_ref, loc.at[6]),
        pltpu.make_async_copy(req_hbm, req_ref, loc.at[7]),
        pltpu.make_async_copy(own_hbm, own_ref, loc.at[8]),
    ]
    local = [
        pltpu.make_async_copy(feat_hbm.at[:, my_cols], halves.at[0, pl.ds(0, crops)], loc.at[0]),
        pltpu.make_async_copy(feat_hbm.at[:, other_cols], halves.at[1, pl.ds(0, crops)], loc.at[1]),
        pltpu.make_async_copy(feat_hbm, feat, loc.at[2]),
        pltpu.make_async_copy(mem_hbm.at[:, my_cols], old.at[0], loc.at[3]),
        pltpu.make_async_copy(mem_hbm.at[:, other_cols], old.at[1], loc.at[4]),
        pltpu.make_async_copy(mem_hbm, gath.at[group], loc.at[5]),
    ]
    tables[0].start()
    local[0].start()
    local[1].start()

    lanes = pair.shape[2]
    pieces = crops // lanes
    square_of = (lanes, lanes)
    sooner = jnp.where(
        lax.broadcasted_iota(jnp.int32, square_of, 0) < lax.broadcasted_iota(jnp.int32, square_of, 1), 1.0, 0.0
    ).astype(BF16)
    pair[0] = jnp.zeros(pair.shape[1:], jnp.int32)
    region_of = lax.broadcasted_iota(jnp.int32, (2 * chips, lanes), 0)
    tables[0].wait()
    split = [lab_ref[:, n * lanes:(n + 1) * lanes] for n in range(pieces)]
    homes = [lax.shift_right_logical(piece, jnp.int32(rows.bit_length() - 1)) for piece in split]
    of_region = [jnp.where(region_of == home, 1.0, 0.0) for home in homes]
    earlier = jnp.dot(
        jnp.concatenate(of_region, axis=0).astype(BF16), sooner, preferred_element_type=F32
    )
    seen = jnp.zeros((2 * chips, 1), F32)
    for n in range(pieces):
        rank = jnp.sum(
            (earlier[n * 2 * chips:(n + 1) * 2 * chips] + seen) * of_region[n], axis=0, keepdims=True
        ).astype(jnp.int32)
        seen += jnp.sum(of_region[n], axis=1, keepdims=True)
        pair[0, n:n + 1, :] = split[n]
        pair[0, pieces + n:pieces + n + 1, :] = homes[n] * slots + rank

    def row_of(tiles, k, first):
        return jnp.concatenate([tiles[k, first + n:first + n + 1, :] for n in range(pieces)], axis=1)

    def labels_of(tiles, k):
        return row_of(tiles, k, 0)

    def slots_of(tiles, k):
        return row_of(tiles, k, pieces)

    pl.semaphore_wait(barrier, len(partners))

    def remote(src, dst, send, recv, device):
        return pltpu.make_async_remote_copy(
            src_ref=src, dst_ref=dst, send_sem=send, recv_sem=recv, device_id=device, device_id_type=MESH
        )

    sibling = dev(chip, other, group)
    swap = [
        remote(pair.at[0], pair.at[1], sib_send.at[0], sib_recv.at[0], sibling),
        remote(feat_hbm.at[:, other_cols], halves.at[0, pl.ds(crops, crops)], sib_send.at[1], sib_recv.at[1], sibling),
        remote(feat_hbm.at[:, my_cols], halves.at[1, pl.ds(crops, crops)], sib_send.at[1], sib_recv.at[2], sibling),
    ]
    swap[0].start()

    def tile_copy(arm, e):
        towards = sign * (1 - 2 * arm) * (1 - 2 * e)
        return remote(
            pair.at[0], labs.at[arm, 0, e], lab_send.at[0], lab_recv.at[arm, 0],
            dev(chip_at(towards), core + e * sign, group),
        )

    def tiles_copy(arm):
        towards = sign * (1 - 2 * arm)
        return remote(
            labs.at[arm, 0], labs.at[arm, 1], lab_send.at[0], lab_recv.at[arm, 1],
            dev(chip_at(towards), core, group),
        )

    for arm in range(2):
        for e in range(2):
            tile_copy(arm, e).start()

    def pack_copy(stage, arm, e):
        towards = sign * (1 - 2 * arm) * (1 - 2 * e)
        place = pl.ds(pl.multiple_of(e * packed, packed), packed)
        landing = near if stage == 0 else far
        return remote(
            packs.at[stage, arm, e], landing.at[arm, place],
            pack_send.at[0], pack_recv.at[arm, stage],
            dev(chip_at(towards), core + e * sign, group),
        )

    def forward_copy(arm):
        towards = sign * (1 - 2 * arm)
        return remote(
            near.at[arm], far.at[arm, pl.ds(2 * packed, 2 * packed)], pack_send.at[1], pack_recv.at[arm, 1],
            dev(chip_at(towards), core, group),
        )

    def packs_here(arm, stage):
        landing = (near if stage == 0 else far).at[arm]
        return remote(landing, landing, pack_send.at[0], pack_recv.at[arm, stage], sibling)

    def send_packed(stage, arm):
        @pl.loop(0, 2)
        def _(e):
            towards = sign * (1 - 2 * arm) * (1 - 2 * e)
            goal = chip_at(towards * (long_arm - arm - stage))
            take = jnp.where(
                lax.broadcasted_iota(jnp.int32, (packed, crops), 0) + goal * packed == slots_of(pair, 0),
                1.0, 0.0,
            ).astype(BF16)
            packs[stage, arm, e] = jnp.dot(
                take, halves[e, 0:crops, :], preferred_element_type=F32
            ).astype(BF16)
            pack_copy(stage, arm, e).start()

    local[0].wait()
    local[1].wait()
    send_packed(0, 0)
    swap[1].start()
    send_packed(1, 0)
    send_packed(0, 1)
    swap[2].start()
    for copy in local[2:] + tables[1:]:
        copy.start()

    offs = (0, -1, 1, 2)

    def block(h, i, j):
        def off(k):
            return k
        dx, dy = (i, j) if h == 0 else (j, i)
        return at_xy(dx, dy)

    def ag_copy(h, kind, src_block, rows_of, device_block, own=False):
        cols = pl.ds(h * half, half)
        dst = gath.at[src_block, rows_of, cols]
        src = mem_hbm.at[rows_of, cols] if own else dst
        return remote(src, dst, ag_send.at[kind], ag_recv.at[kind], (region, device_block))

    full = pl.ds(0, rows)
    part_of = {1: pl.ds(0, rows // 2), -1: pl.ds(rows // 2, rows // 2)}

    def p1(h, u, recv=False):
        return ag_copy(h, 0, block(h, -u, 0) if recv else block(h, 0, 0), full, block(h, u, 0), own=not recv)

    def p2(h, u, recv=False):
        return ag_copy(h, 1, block(h, -2 * u if recv else -u, 0), part_of[u], block(h, u, 0))

    def q1(h, a, u, recv=False):
        return ag_copy(
            h, (2, 3, 3, 4)[a], block(h, offs[a], -u if recv else 0), full, block(h, 0, u), own=(a == 0 and not recv)
        )

    def q2(h, a, u, recv=False):
        return ag_copy(
            h, 5, block(h, offs[a], -2 * u if recv else -u), part_of[u], block(h, 0, u)
        )

    both = (1, -1)

    def gather_round0():
        for u in both:
            for h in range(2):
                p1(h, u).start()
        for u in both:
            for h in range(2):
                q1(h, 0, u).start()

    amounts = (2, 1, 2, 4, 2, 4)

    def whole(kind):
        some = gath.at[pl.ds(0, amounts[kind])]
        return remote(some, some, ag_send.at[kind], ag_recv.at[kind], sibling)

    def gather_round1():
        whole(0).wait_recv()
        for h in range(2):
            for u, a in ((1, 1), (-1, 2)):
                p2(h, u).start()
                for v in both:
                    q1(h, a, v).start()

    def gather_round1b():
        whole(2).wait_recv()
        for h in range(2):
            for u in both:
                q2(h, 0, u).start()

    def gather_round2():
        whole(1).wait_recv()
        for h in range(2):
            for u in both:
                q1(h, 3, u).start()
        whole(3).wait_recv()
        for h in range(2):
            for a in (1, 2):
                for u in both:
                    q2(h, a, u).start()

    def gather_round3():
        whole(4).wait_recv()
        for h in range(2):
            for u in both:
                q2(h, 3, u).start()

    def gather_round4():
        whole(5).wait_recv()
        local[5].wait()

    def gather_sent():
        for kind in range(len(amounts)):
            whole(kind).wait_send()

    gather_round0()

    places = lax.broadcasted_iota(jnp.int32, (rows, crops), 0)

    def hit(label_row, target):
        return jnp.where(places == label_row - target * rows, 1.0, 0.0)

    def own_pick(target):
        return jnp.concatenate([hit(labels_of(pair, k), target) for k in range(2)], axis=1).astype(BF16)

    def own_sums(pick, which):
        return jnp.dot(pick, halves[which], preferred_element_type=F32)

    def tally(pick):
        ones = jnp.ones((8, pick.shape[1]), BF16)
        return lax.dot_general(ones, pick, (((1,), (1,)), ((), ())), preferred_element_type=F32)[0:1]

    def moves(arm, target):
        sources = [(labs.at[arm, hop], k) for hop in range(2) for k in range(2)]
        first = target // 2 * packed
        put, take = [], []
        for n, (source, k) in enumerate(sources):
            slot = slots_of(source, k) - first
            slot = jnp.where((slot >= 0) & (slot < packed), slot + n * packed, -1)
            place = lax.broadcasted_iota(jnp.int32, (4 * packed, crops), 0)
            take.append(jnp.where(place == slot, 1.0, 0.0).astype(BF16))
            put.append(hit(labels_of(source, k), target).astype(BF16))
        put = jnp.concatenate(put, axis=1)
        through = lax.dot_general(
            put, jnp.concatenate(take, axis=1), (((1,), (1,)), ((), ())), preferred_element_type=F32
        )
        return through.astype(BF16), tally(put)

    def ring_copy(t, arm, e, device):
        return remote(
            ring.at[arm, e, t - 2], ring.at[arm, e, t - 1], ring_send.at[arm], ring_recv.at[arm, e, t - 2],
            device,
        )

    def last_copy(e, r):
        span = pl.ds(r * (rows // 2), rows // 2)
        _, nearest = ring_target(long_arm - 1, 0, e)
        return remote(
            ring.at[0, e, long_arm - 3, span], ring.at[0, e, long_arm - 2, span], ring_send.at[0], last_recv.at[e, r],
            nearest,
        )

    def ring_target(t, arm, e):
        towards = sign * (1 - 2 * arm)
        distance = long_arm - arm - t
        goal = chip_at(towards * distance) * 2 + core + e * sign
        last = (t + arm) // (long_arm - 1)
        nearest = dev(chip_at(towards), core + last * e * sign, group)
        return goal, nearest

    def tally_copy(t, arm):
        towards = sign * (1 - 2 * arm)
        return remote(
            tallies.at[arm, t - 2], tallies.at[arm, t - 1], tally_send.at[arm], tally_recv.at[arm, t - 2],
            dev(chip_at(towards), core, group),
        )

    for arm in range(2):
        remote(pair, labs.at[arm, 0], lab_send.at[0], lab_recv.at[arm, 0], sibling).wait_recv()
        tiles_copy(arm).start()
    swap[0].wait_recv()

    def take_candidates():
        tables[1].wait()
        tables[2].wait()
        for k in range(8):
            cand[k * rows:(k + 1) * rows, :] = gath[own_ref[0, req_ref[0, k]]]

    def scores():
        local[2].wait()

        @pl.loop(0, 4)
        def _(n):
            span = pl.ds(pl.multiple_of(n * 256, 256), 256)
            score[:, span] = lax.dot_general(
                feat[...], cand[span, :], (((1,), (1,)), ((), ())), preferred_element_type=F32
            ) * (1.0 / SHARPNESS)

    def softmax():
        total = cand.shape[0]

        @pl.loop(0, crops // 64)
        def _(n):
            span = pl.ds(pl.multiple_of(n * 64, 64), 64)
            s = score[span, :]
            expo = jnp.exp(s - jnp.max(s, axis=1, keepdims=True))
            prob = expo / jnp.sum(expo, axis=1, keepdims=True)
            column = lax.broadcasted_iota(jnp.int32, s.shape, 1)
            target = jnp.where(column < rows, (1.0 - SMOOTHING) / rows, 0.0) + SMOOTHING / total
            logit[span, :] = ((prob - target) * (1.0 / SHARPNESS)).astype(BF16)

    def grads():
        @pl.loop(0, width // 256)
        def _(n):
            span = pl.ds(pl.multiple_of(n * 256, 256), 256)
            grad[:, span] = jnp.dot(logit[...], cand[:, span], preferred_element_type=F32).astype(BF16)

    for arm in range(2):
        packs_here(arm, 0).wait_recv()
        forward_copy(arm).start()
        if arm == 0:
            send_packed(1, 1)
    swap[1].wait_recv()

    for arm in range(2):
        @pl.loop(0, 2)
        def _(e):
            goal, _ = ring_target(2, arm, e)
            part[2 * arm + e] = own_sums(own_pick(goal), 0)

        if arm == 0:
            gather_round1()
        tiles_copy(arm).wait_recv()

        @pl.loop(0, 2)
        def _(e):
            goal, _ = ring_target(2, arm, e)
            through, number = moves(arm, goal)
            move[2 * arm + e] = through

            @pl.when(e == 0)
            def _():
                tallies[arm, 0] = number + tally(own_pick(goal))
                tally_copy(2, arm).start()

        packs_here(arm, 1).wait_recv()

        @pl.loop(0, 2)
        def _(e):
            _, nearest = ring_target(2, arm, e)
            come = jnp.dot(move[2 * arm + e], far[arm], preferred_element_type=F32)
            ring[arm, e, 0] = (part[2 * arm + e] + come).astype(BF16)
            ring_copy(2, arm, e, nearest).start()

    gather_round1b()

    @pl.loop(3, long_arm - 1)
    def _(t):
        @pl.loop(0, 4)
        def _(q):
            arm, e = q // 2, q % 2
            goal, nearest = ring_target(t, arm, e)
            pick = own_pick(goal)
            part[0] = own_sums(pick, 0)

            @pl.when(e == 0)
            def _():
                number = tally(pick)
                tally_copy(t - 1, arm).wait_recv()
                tallies[arm, t - 2] = tallies[arm, t - 2] + number
                tally_copy(t, arm).start()

            ring_copy(t - 1, arm, e, nearest).wait_recv()
            ring[arm, e, t - 2] = (part[0] + ring[arm, e, t - 2].astype(F32)).astype(BF16)
            ring_copy(t, arm, e, nearest).start()

        @pl.when(t == 3)
        def _():
            gather_round2()

        @pl.when(t == 4)
        def _():
            gather_round3()

        @pl.when(t == 5)
        def _():
            gather_round4()
            take_candidates()
            scores()

        @pl.when(t == 6)
        def _():
            softmax()
            grads()

    for e in range(2):
        goal, _ = ring_target(long_arm - 1, 0, e)
        pick = own_pick(goal)
        part[0] = own_sums(pick, 0)
        if e == 0:
            number = tally(pick)
            tally_copy(long_arm - 2, 0).wait_recv()
            tallies[0, long_arm - 3] = tallies[0, long_arm - 3] + number
            tally_copy(long_arm - 1, 0).start()
        ring_copy(long_arm - 2, 0, e, sibling).wait_recv()
        for r in range(2):
            span = pl.ds(r * (rows // 2), rows // 2)
            ring[0, e, long_arm - 3, span, :] = (
                part[0, span, :] + ring[0, e, long_arm - 3, span, :].astype(F32)
            ).astype(BF16)
            last_copy(e, r).start()

    pick = own_pick(region)
    tally_copy(long_arm - 2, 1).wait_recv()
    tally_copy(long_arm - 1, 0).wait_recv()
    number = tally(pick) + tallies[0, long_arm - 2] + tallies[1, long_arm - 3]
    own_place = (rows, rows)
    diagonal = lax.broadcasted_iota(jnp.int32, own_place, 0) == lax.broadcasted_iota(jnp.int32, own_place, 1)
    counts = jnp.sum(jnp.where(diagonal, number, 0.0), axis=1, keepdims=True)
    keep = jnp.where(counts > 0, KEEP, 1.0)
    take = jnp.where(counts > 0, (1.0 - KEEP) / jnp.maximum(counts, 1.0), 0.0)
    swap[2].wait_recv()
    local[3].wait()
    local[4].wait()
    for which in range(2):
        part[0] = own_sums(pick, which)
        ring_copy(long_arm - 2, 1, which, sibling).wait_recv()
        mix[which] = keep * old[which].astype(F32) + take * (part[0] + ring[1, which, long_arm - 3].astype(F32))
    swap[0].wait_send()
    remote(halves.at[0], halves.at[0], sib_send.at[1], sib_recv.at[1], sibling).wait_send()
    gather_sent()
    remote(packs, packs, pack_send.at[0], pack_recv.at[0, 0], sibling).wait_send()
    remote(near, near, pack_send.at[1], pack_recv.at[0, 0], sibling).wait_send()
    remote(labs, labs, lab_send.at[0], lab_recv.at[0, 0], sibling).wait_send()
    square = [None, None]
    for which, cols in ((0, my_cols), (1, other_cols)):
        for r in range(2):
            span = pl.ds(r * (rows // 2), rows // 2)
            last_copy(which, r).wait_recv()
            mixed = mix[which, span, :] + take[r * (rows // 2):(r + 1) * (rows // 2)] * ring[
                0, which, long_arm - 2, span, :
            ].astype(F32)
            ones = jnp.sum(mixed * mixed, axis=1, keepdims=True)
            if which == 0:
                mix[0, span, :] = mixed
                square[r] = ones
            else:
                scale = lax.rsqrt((square[r] + ones) * (1.0 / width) + 1e-06) * width ** (-0.5)
                new[span, cols] = (mixed * scale).astype(BF16)
                new[span, my_cols] = (mix[0, span, :] * scale).astype(BF16)

    for arm in range(2):
        sent = tallies.at[arm, pl.ds(0, long_arm - 2 - arm)]
        remote(sent, sent, tally_send.at[arm], tally_recv.at[arm, 0], sibling).wait_send()
        sent = ring.at[arm, :, pl.ds(0, long_arm - 2 - arm)]
        remote(sent, sent, ring_send.at[arm], ring_recv.at[arm, 0, 0], sibling).wait_send()


def hand_over(grad, new, grad_out, new_out, sem):
    copies = [
        pltpu.make_async_copy(grad, grad_out, sem.at[0]),
        pltpu.make_async_copy(new, new_out, sem.at[1]),
    ]
    for copy in copies:
        copy.start()
    for copy in copies:
        copy.wait()


def solution(mesh):
    regions, groups = mesh.shape["region"], mesh.shape["group"]
    chips = regions // 2
    side = int(round(groups ** 0.5))

    def on_device(features, memory, requests, owners, labels):
        crops, width = features.shape
        rows = memory.shape[0]
        half = width // 2
        arm = chips // 2
        total = requests.shape[1] * rows
        any_spec = pl.BlockSpec(memory_space=pl.ANY)
        vmem = pl.BlockSpec(memory_space=pltpu.VMEM)
        dma = pltpu.SemaphoreType.DMA
        packed = 2 * max(2, 2 * crops // regions)
        results = pl.pallas_call(
            functools.partial(kernel, chips, side),
            out_shape=(pltpu.VMEM((crops, width), BF16), pltpu.VMEM((rows, width), BF16)),
            in_specs=[any_spec] * 5,
            out_specs=(vmem, vmem),
            scratch_shapes=[
                pltpu.SMEM(requests.shape, jnp.int32),
                pltpu.SMEM(owners.shape, jnp.int32),
                pltpu.VMEM(labels.shape, jnp.int32),
                pltpu.VMEM((crops, width), BF16),
                pltpu.VMEM((2, 2 * crops, half), BF16),
                pltpu.VMEM((2, 2, arm - 1, rows, half), BF16),
                pltpu.VMEM((2, 2, 2, packed, half), BF16),
                pltpu.VMEM((2, 2 * packed, half), BF16),
                pltpu.VMEM((2, 4 * packed, half), BF16),
                pltpu.VMEM((2, 8, 128), jnp.int32),
                pltpu.VMEM((2, 2, 2, 8, 128), jnp.int32),
                pltpu.VMEM((2, arm - 1, 1, rows), F32),
                pltpu.VMEM((groups, rows, width), BF16),
                pltpu.VMEM((2, rows, half), BF16),
                pltpu.VMEM((4, rows, half), F32),
                pltpu.VMEM((4, rows, 4 * packed), BF16),
                pltpu.VMEM((total, width), BF16),
                pltpu.VMEM((crops, total), F32),
                pltpu.VMEM((crops, total), BF16),
                pltpu.VMEM((2, rows, half), F32),
                dma((2,)),
                dma((2, 2, arm - 3)),
                dma((2,)),
                dma((2, 2)),
                dma((1,)),
                dma((2, 2)),
                dma((2,)),
                dma((2, arm - 2)),
                dma((2,)),
                dma((3,)),
                dma((6,)),
                dma((6,)),
                dma((2, 2)),
                dma((9,)),
            ],
            compiler_params=pltpu.CompilerParams(
                collective_id=0, has_side_effects=True, vmem_limit_bytes=56 << 20
            ),
        )(features, memory, requests, owners, labels)
        results = [pltpu.with_memory_space_constraint(r, pltpu.VMEM) for r in results]
        return pl.pallas_call(
            hand_over,
            out_shape=(
                jax.ShapeDtypeStruct((crops, width), BF16),
                jax.ShapeDtypeStruct((rows, width), BF16),
            ),
            in_specs=[vmem, vmem],
            out_specs=(any_spec, any_spec),
            scratch_shapes=[dma((2,))],
        )(*results)

    both = P(("region", "group"), None)
    return jax.shard_map(
        on_device,
        mesh=mesh,
        in_specs=(both, both, both, P("region", None), both),
        out_specs=(both, both),
        check_vma=False,
    )
```
